32 devices in a mesh: probe: 2 (over x), space: 16 (over z, y, core).
Axes of the slice: x: 2, y: 2, z: 4, core: 2. Of those that a mesh axis runs over, the one named last changes fastest.
Arguments:
- field_before: float32 [2, 64, 256, 256], P('probe', 'space'), may hold values from -6 to 6
- field_now: float32 [2, 64, 256, 256], P('probe', 'space'), may hold values from -6 to 6
- stiffness: float32 [64, 256, 256], P('space'), may hold values from 0.04 to 0.1
- buoyancy: float32 [64, 256, 256], P('space'), may hold values from 0.6 to 1.4
- perturbation: float32 [2, 64, 256, 256], P('probe', 'space'), may hold values from -0.25 to 0.25
Outputs:
- field_after: float32 [2, 64, 256, 256], P('probe', 'space')
The draws below stay inside these ranges and needn't reach their ends.
All inputs are finite; a program needn't handle non-finite values.
Results may differ from the reference program's by a relative error of at most 0.00002.
Values sent between devices are 32-bit elements; how exact they have to be, the bound alone decides.
No kernel may reach another device: no remote copies, remote signals or barrier semaphores. Data moves between devices by JAX's collectives and lax.ppermute only.
A program may use at most 128 MiB of HBM per device.

```python
import jax
import jax.numpy as jnp
from jax import lax

NY = 256
NZ = 256
STEPS = 2
NX = 64
GROUPS = 2


def shard_levels(rng, dims, shards, low, top_value):
    def one(axis_at, blocks):
        heights = jax.random.uniform(jax.random.fold_in(jax.random.fold_in(rng, 6), axis_at), (blocks,), jnp.float32, low / len(shards), top_value / len(shards))
        return jnp.repeat(jnp.exp(heights), dims[axis_at] // blocks).reshape((-1,) + (1,) * (len(dims) - axis_at - 1))

    factor_of = one(*shards[0])
    for cut in shards[1:]:
        factor_of = factor_of * one(*cut)
    return factor_of


def noise(stream_key, shape, deviation, limit, cuts=(), dtype=jnp.bfloat16):
    result = deviation * jax.random.normal(stream_key, shape, jnp.float32)
    if cuts:
        result = result * shard_levels(stream_key, shape, cuts, -0.22, 0.18)
    return jnp.clip(result, -limit, limit).astype(dtype)


def setup_inputs(seed: int = 0) -> dict:
    key_list = jax.random.split(jax.random.key(seed), 6)
    return {
        "field_before": noise(key_list[0], (GROUPS, NX, NY, NZ), 1.0, 6.0, ((0, 2), (1, 16)), jnp.float32),
        "field_now": noise(key_list[1], (GROUPS, NX, NY, NZ), 1.0, 6.0, ((0, 2), (1, 16)), jnp.float32),
        "stiffness": jnp.clip(0.04 + 0.060000002 * jax.random.uniform(key_list[2], (NX, NY, NZ), jnp.float32) ** shard_levels(key_list[2], (NX, NY, NZ), ((0, 16),), -0.2, 0.2), 0.04, 0.1),
        "buoyancy": jnp.clip(0.6 + 0.79999995 * jax.random.uniform(key_list[3], (NX, NY, NZ), jnp.float32) ** shard_levels(key_list[3], (NX, NY, NZ), ((0, 16),), -0.2, 0.2), 0.6, 1.4),
        "perturbation": noise(key_list[4], (GROUPS, NX, NY, NZ), 0.05, 0.25, ((0, 2), (1, 16)), jnp.float32),
    }


second_coeffs = (8.0 / 5.0, -1.0 / 5.0, 8.0 / 315.0, -1.0 / 560.0)
first_coeffs = (4.0 / 5.0, -1.0 / 5.0, 4.0 / 105.0, -1.0 / 280.0)
centre_coeff = -205.0 / 72.0


def shifted(padded, direction, offset):
    window = [slice(4, padded.shape[0] - 4), slice(4, padded.shape[1] - 4), slice(4, padded.shape[2] - 4)]
    window[direction] = slice(4 + offset, padded.shape[direction] - 4 + offset)
    return padded[tuple(window)]


def second_sum(padded):
    total = 3.0 * centre_coeff * shifted(padded, 0, 0)
    for direction in range(3):
        for reach in range(1, 5):
            total = total + second_coeffs[reach - 1] * (shifted(padded, direction, reach) + shifted(padded, direction, -reach))
    return total


def first_parts(padded):
    parts = []
    for direction in range(3):
        total = jnp.zeros_like(shifted(padded, 0, 0))
        for reach in range(1, 5):
            total = total + first_coeffs[reach - 1] * (shifted(padded, direction, reach) - shifted(padded, direction, -reach))
        parts.append(total)
    return parts


def divergence(padded, buoyancy, slope):
    grads = first_parts(padded)
    return buoyancy * second_sum(padded) + slope[0] * grads[0] + slope[1] * grads[1] + slope[2] * grads[2]


def reference(field_before, field_now, stiffness, buoyancy, perturbation):
    slope = first_parts(jnp.pad(buoyancy - 1.0, 4))

    def operate(field):
        return divergence(jnp.pad(field, 4), buoyancy, slope)

    born_flag = (jnp.arange(GROUPS) > 0).astype(jnp.float32)[:, None, None, None]
    before, now = field_before, field_now
    for step in range(STEPS):
        images = lax.map(operate, now)
        following = 2.0 * now - before + stiffness[None] * images + born_flag * perturbation * images[0][None]
        before, now = now, following
    return now
```

```python
import functools

import jax
import jax.numpy as jnp
from jax import lax
from jax.experimental import pallas as pl
from jax.experimental.pallas import tpu as pltpu
from jax.sharding import PartitionSpec as P

STEPS = 2
REACH = 4
SUB = 8
LANES = 128

second_coeffs = (8.0 / 5.0, -1.0 / 5.0, 8.0 / 315.0, -1.0 / 560.0)
first_coeffs = (4.0 / 5.0, -1.0 / 5.0, 4.0 / 105.0, -1.0 / 280.0)
centre_coeff = -205.0 / 72.0


def pad_copy(scratch, pieces, width):
    for scr, load in pieces:
        planes, halves = scr.shape[0], scr.shape[1]
        zero = jnp.zeros((planes, SUB, LANES), jnp.float32)
        for h in range(halves):
            scr[:, h, pl.ds(0, SUB), :] = zero
            scr[:, h, pl.ds(width + SUB, SUB), :] = zero

    def body(i, _):
        for scr, load in pieces:
            value = load(i)
            for h in range(scr.shape[1]):
                scr[:, h, pl.ds(pl.multiple_of(SUB * (i + 1), SUB), SUB), :] = value[:, :, h * LANES:(h + 1) * LANES]
        return 0

    lax.fori_loop(0, width // SUB, body, 0)


def taps(scr, row, low, high, h, lane):
    halves = scr.shape[1]
    here = [scr[:, j, pl.ds(pl.multiple_of(row, SUB), SUB), :] for j in range(halves)]
    centre = here[h]
    slab = centre.shape[0]
    full = jnp.concatenate([low, centre, high], axis=0)
    out = []
    for k in range(1, REACH + 1):
        first = (full[REACH + k:REACH + k + slab], full[REACH - k:REACH - k + slab])
        second = (scr[:, h, pl.ds(row + k, SUB), :], scr[:, h, pl.ds(row - k, SUB), :])
        up = pltpu.roll(centre, LANES - k, 2)
        down = pltpu.roll(centre, k, 2)
        above = pltpu.roll(here[h + 1], LANES - k, 2) if h + 1 < halves else 0.0
        below = pltpu.roll(here[h - 1], k, 2) if h > 0 else 0.0
        third = (jnp.where(lane < LANES - k, up, above), jnp.where(lane >= k, down, below))
        out.append((first, second, third))
    return centre, out


def firsts(near):
    totals = []
    for d in range(3):
        total = None
        for k in range(REACH):
            term = first_coeffs[k] * (near[k][d][0] - near[k][d][1])
            total = term if total is None else total + term
        totals.append(total)
    return totals


def seconds(centre, near):
    total = (3.0 * centre_coeff) * centre
    for k in range(REACH):
        (a, b), (c, d), (e, f) = near[k]
        total = total + second_coeffs[k] * (((a + b) + (c + d)) + (e + f))
    return total


def sides(even, inner, outer):
    return jnp.where(even, outer, inner), jnp.where(even, inner, outer)


def lane_index(slab):
    return lax.broadcasted_iota(jnp.int32, (slab, SUB, LANES), 2)


def slope_kernel(width, info, buoy, inner, outer, s1, s2, s3, scr):
    start, even = info[0], info[1] == 1
    slab, halves = scr.shape[0], scr.shape[1]

    def load(i):
        return buoy[:, pl.ds(pl.multiple_of(start + SUB * i, SUB), SUB), :] - 1.0

    pad_copy(None, [(scr, load)], width)
    lane = lane_index(slab)

    def body(i, _):
        rows = pl.ds(pl.multiple_of(SUB * i, SUB), SUB)
        for h in range(halves):
            cols = slice(h * LANES, (h + 1) * LANES)
            low, high = sides(even, inner[0, :, rows, cols], outer[0, :, rows, cols])
            _, near = taps(scr, SUB * (i + 1), low, high, h, lane)
            for ref, value in zip((s1, s2, s3), firsts(near)):
                ref[:, rows, cols] = value
        return 0

    lax.fori_loop(0, width // SUB, body, 0)


def operator(scr, row, low, high, h, lane, buoyancy, slopes):
    centre, near = taps(scr, row, low, high, h, lane)
    grads = firsts(near)
    value = buoyancy * seconds(centre, near)
    for slope, grad in zip(slopes, grads):
        value = value + slope * grad
    return centre, value


def first_kernel(parts, width, rows_core, info, now_own, now_far, in_own, out_own, in_far, out_far, before_own, far,
                 pert_own, stiff, buoy, s1, s2, s3, following, faces, *scrs):
    start, even, base, offset = info[0], info[1] == 1, info[2], info[3]
    slab, halves = scrs[0].shape[0], scrs[0].shape[1]

    def whole(i):
        return pl.ds(pl.multiple_of(start + SUB * i, SUB), SUB)

    loads = [lambda i: now_own[:, whole(i), :]]
    for s in range(1, parts):
        loads.append(lambda i, s=s: now_far[s - 1, :, pl.ds(pl.multiple_of(SUB * i, SUB), SUB), :])
    pad_copy(None, list(zip(scrs, loads)), width)
    lane = lane_index(slab)

    def body(i, _):
        rows = pl.ds(pl.multiple_of(SUB * i, SUB), SUB)
        for h in range(halves):
            cols = slice(h * LANES, (h + 1) * LANES)
            slopes = [ref[:, rows, cols] for ref in (s1, s2, s3)]
            b = buoy[:, whole(i), cols]
            k = stiff[:, whole(i), cols]
            centres, images = [], []
            for s in range(parts):
                if s == 0:
                    low, high = sides(even, in_own[1, :, rows, cols], out_own[1, :, rows, cols])
                else:
                    low, high = sides(even, in_far[s - 1, :, rows, cols], out_far[s - 1, :, rows, cols])
                centre, image = operator(scrs[s], SUB * (i + 1), low, high, h, lane, b, slopes)
                centres.append(centre)
                images.append(image)
            source = images[0]
            for s in range(1, parts):
                source = jnp.where(base == s, images[s], source)
            for s in range(parts):
                if s == 0:
                    before = before_own[:, whole(i), cols]
                    scale = pert_own[:, whole(i), cols]
                else:
                    before = far[s - 1, 0, :, rows, cols]
                    scale = far[s - 1, 1, :, rows, cols]
                scale = jnp.where(base == s, 0.0, scale)
                value = 2.0 * centres[s] - before + k * images[s] + scale * source
                following[s, :, rows, cols] = value
        return 0

    lax.fori_loop(0, width // SUB, body, 0)

    def core(i, _):
        src = pl.ds(pl.multiple_of(offset + SUB * i, SUB), SUB)
        dst = pl.ds(pl.multiple_of(SUB * i, SUB), SUB)
        faces[:, :, dst, :] = following[:, :, src, :]
        return 0

    lax.fori_loop(0, rows_core // SUB, core, 0)


def second_kernel(parts, width, rows_core, info, now, inner, outer, before_own, before_far, far, pert_own, stiff, buoy,
                  s1, s2, s3, own, others, *scrs):
    start, even, base, offset = info[0], info[1] == 1, info[2], info[3]
    slab, halves = scrs[0].shape[0], scrs[0].shape[1]
    loads = []
    for s in range(parts):
        loads.append(lambda i, s=s: now[s, :, pl.ds(pl.multiple_of(SUB * i, SUB), SUB), :])
    pad_copy(None, list(zip(scrs, loads)), width)
    lane = lane_index(slab)

    def body(i, _):
        rows = pl.ds(pl.multiple_of(SUB * i, SUB), SUB)
        win = pl.ds(pl.multiple_of(offset + SUB * i, SUB), SUB)
        whole = pl.ds(pl.multiple_of(start + offset + SUB * i, SUB), SUB)
        for h in range(halves):
            cols = slice(h * LANES, (h + 1) * LANES)
            slopes = [ref[:, win, cols] for ref in (s1, s2, s3)]
            b = buoy[:, whole, cols]
            k = stiff[:, whole, cols]
            centres, images = [], []
            for s in range(parts):
                low, high = sides(even, inner[s, :, rows, cols], outer[s, :, rows, cols])
                centre, image = operator(scrs[s], offset + SUB * (i + 1), low, high, h, lane, b, slopes)
                centres.append(centre)
                images.append(image)
            source = images[0]
            for s in range(1, parts):
                source = jnp.where(base == s, images[s], source)
            for s in range(parts):
                if s == 0:
                    before = before_own[:, whole, cols]
                    scale = pert_own[:, whole, cols]
                else:
                    before = before_far[s - 1, :, win, cols]
                    scale = far[s - 1, 1, :, win, cols]
                scale = jnp.where(base == s, 0.0, scale)
                value = 2.0 * centres[s] - before + k * images[s] + scale * source
                if s == 0:
                    own[:, whole, cols] = value
                else:
                    others[s - 1, :, rows, cols] = value
        return 0

    lax.fori_loop(0, rows_core // SUB, body, 0)


def call(kernel, info, args, outs, scratch, flops):
    vmem = pl.BlockSpec(memory_space=pltpu.VMEM)
    size = sum(4 * a.size for a in args) + sum(4 * o.size for o in outs)
    return pl.pallas_call(
        kernel,
        out_shape=outs,
        in_specs=[pl.BlockSpec(memory_space=pltpu.SMEM)] + [vmem] * len(args),
        out_specs=[vmem] * len(outs),
        scratch_shapes=scratch,
        compiler_params=pltpu.CompilerParams(vmem_limit_bytes=24 << 20),
        cost_estimate=pl.CostEstimate(flops=flops, bytes_accessed=size, transcendentals=0),
    )(info, *args)


def on_device(field_before, field_now, stiffness, buoyancy, perturbation):
    parts, count = lax.axis_size("probe"), lax.axis_size("space")
    part, place = lax.axis_index("probe"), lax.axis_index("space")
    before, now, pert = field_before[0], field_now[0], perturbation[0]
    slab, height, depth = now.shape
    core = height // parts
    width = min(height, core + (2 if parts > 2 else 1) * 2 * REACH)

    def window(p):
        return jnp.clip(core * p - 2 * REACH, 0, height - width)

    start = window(part)
    offset = core * part - start
    even = place % 2 == 0
    info = jnp.stack([start, even.astype(jnp.int32), part, offset]).astype(jnp.int32)

    def rows(field, p):
        return lax.dynamic_slice_in_dim(field, window(p), width, axis=field.ndim - 2)

    inner_pairs = [(i, i ^ 1) for i in range(count)]
    outer_pairs = [(i, ((i + 1) ^ 1) - 1) for i in range(1, count - 1)]

    def exchange(stack):
        results = []
        for pairs, from_end in ((inner_pairs, even), (outer_pairs, jnp.logical_not(even))):
            face = stack
            if slab > REACH:
                face = lax.dynamic_slice_in_dim(stack, jnp.where(from_end, slab - REACH, 0), REACH, axis=1)
            results.append(lax.ppermute(face, "space", pairs))
        return results

    def turn(field, s):
        return lax.ppermute(field, "probe", [(i, (i + s) % parts) for i in range(parts)])

    in_own, out_own = exchange(jnp.stack([rows(buoyancy, part) - 1.0, rows(now, part)]))
    now_far = jnp.stack([turn(rows(now, (part + s) % parts), s) for s in range(1, parts)])
    in_far, out_far = exchange(now_far)
    pair = lax.optimization_barrier((before, pert, now_far))
    far = jnp.stack(
        [turn(rows(jnp.stack([pair[0], pair[1]]), (part + s) % parts), s) for s in range(1, parts)]
    )

    f32 = jnp.float32
    field = jax.ShapeDtypeStruct((slab, width, depth), f32)
    scr = pltpu.VMEM((slab, depth // LANES, width + 2 * SUB, LANES), f32)
    cells = slab * width * depth
    s1, s2, s3 = call(
        functools.partial(slope_kernel, width), info, (buoyancy, in_own, out_own), [field] * 3, [scr], 33 * cells
    )
    following, faces = call(
        functools.partial(first_kernel, parts, width, core),
        info,
        (now, now_far, in_own, out_own, in_far, out_far, before, far, pert, stiffness, buoyancy, s1, s2, s3),
        [
            jax.ShapeDtypeStruct((parts, slab, width, depth), f32),
            jax.ShapeDtypeStruct((parts, slab, core, depth), f32),
        ],
        [scr] * parts,
        80 * parts * cells,
    )
    inner, outer = exchange(faces)
    own, others = call(
        functools.partial(second_kernel, parts, width, core),
        info,
        (following, inner, outer, now, now_far, far, pert, stiffness, buoyancy, s1, s2, s3),
        [
            jax.ShapeDtypeStruct((slab, height, depth), f32),
            jax.ShapeDtypeStruct((parts - 1, slab, core, depth), f32),
        ],
        [scr] * parts,
        80 * parts * cells,
    )
    for s in range(1, parts):
        back = turn(others[s - 1], parts - s)
        own = lax.dynamic_update_slice_in_dim(own, back, core * ((part + s) % parts), axis=1)
    return own[None]


def solution(mesh):
    placed = (
        P("probe", "space", None, None),
        P("probe", "space", None, None),
        P("space", None, None),
        P("space", None, None),
        P("probe", "space", None, None),
    )
    return jax.shard_map(
        on_device,
        mesh=mesh,
        in_specs=placed,
        out_specs=P("probe", "space", None, None),
        check_vma=False,
    )
```

```python
import functools

import jax
import jax.numpy as jnp
from jax import lax
from jax.experimental import pallas as pl
from jax.experimental.pallas import tpu as pltpu
from jax.sharding import PartitionSpec as P

STEPS = 2
REACH = 4
SUB = 8
LANES = 128
HALF = (1, 2)
TINY = True

second_coeffs = (8.0 / 5.0, -1.0 / 5.0, 8.0 / 315.0, -1.0 / 560.0)
first_coeffs = (4.0 / 5.0, -1.0 / 5.0, 4.0 / 105.0, -1.0 / 280.0)
centre_coeff = -205.0 / 72.0


def aligned(row):
    return pl.ds(pl.multiple_of(row, SUB), SUB)


def total_of(terms):
    total = None
    for term in terms:
        total = term if total is None else total + term
    return total


def pad_rows(scr, load, width):
    planes, halves = scr.shape[0], scr.shape[1]
    zero = jnp.zeros((planes, SUB, LANES), jnp.float32)
    for h in range(halves):
        scr[:, h, pl.ds(0, SUB), :] = zero
        scr[:, h, pl.ds(width + SUB, SUB), :] = zero

    def body(i, _):
        value = load(SUB * i)
        for h in range(halves):
            scr[:, h, aligned(SUB * (i + 1)), :] = value[:, :, h * LANES:(h + 1) * LANES]
        return 0

    lax.fori_loop(0, width // SUB, body, 0)


def local_terms(scr, row, h, lane, with_second=True):
    halves = scr.shape[1]
    here = [scr[:, j, aligned(row + SUB), :] for j in range(halves)]
    centre = here[h]
    slab = centre.shape[0]
    grads = ([], [])
    laps = []
    for k in range(1, REACH + 1):
        up = pltpu.roll(centre, LANES - k, 2)
        down = pltpu.roll(centre, k, 2)
        above = pltpu.roll(here[h + 1], LANES - k, 2) if h + 1 < halves else 0.0
        below = pltpu.roll(here[h - 1], k, 2) if h > 0 else 0.0
        up = jnp.where(lane < LANES - k, up, above)
        down = jnp.where(lane >= k, down, below)
        right = scr[:, h, pl.ds(row + SUB + k, SUB), :]
        left = scr[:, h, pl.ds(row + SUB - k, SUB), :]
        grads[0].append(first_coeffs[k - 1] * (right - left))
        grads[1].append(first_coeffs[k - 1] * (up - down))
        if with_second:
            laps.append(second_coeffs[k - 1] * ((right + left) + (up + down)))
    planes = []
    plane_laps = []
    for p in range(slab):
        first, second = [], []
        for k in range(1, REACH + 1):
            high = centre[p + k] if p + k < slab else None
            low = centre[p - k] if p >= k else None
            if high is not None and low is not None:
                first.append(first_coeffs[k - 1] * (high - low))
                second.append(second_coeffs[k - 1] * (high + low))
            elif high is not None:
                first.append(first_coeffs[k - 1] * high)
                second.append(second_coeffs[k - 1] * high)
            elif low is not None:
                first.append(-first_coeffs[k - 1] * low)
                second.append(second_coeffs[k - 1] * low)
        planes.append(total_of(first))
        plane_laps.append(total_of(second))
    along = jnp.stack(planes)
    lap = None
    if with_second:
        lap = total_of(laps + [(3.0 * centre_coeff) * centre, jnp.stack(plane_laps)])
    return centre, lap, along, total_of(grads[0]), total_of(grads[1])


def face_terms(low, high, slab, with_second=True):
    laps, grads = [], []
    for p in range(slab):
        first, second = [], []
        for k in range(1, REACH + 1):
            if p + k >= slab:
                plane = high[p + k - slab]
                first.append(first_coeffs[k - 1] * plane)
                second.append(second_coeffs[k - 1] * plane)
            if p - k < 0:
                plane = low[REACH + p - k]
                first.append(-first_coeffs[k - 1] * plane)
                second.append(second_coeffs[k - 1] * plane)
        zero = jnp.zeros_like(low[0])
        grads.append(total_of(first) if first else zero)
        laps.append(total_of(second) if second else zero)
    return (jnp.stack(laps) if with_second else None), jnp.stack(grads)


def lane_index(slab):
    return lax.broadcasted_iota(jnp.int32, (slab, SUB, LANES), 2)


def columns(depth):
    return [slice(h * LANES, (h + 1) * LANES) for h in range(depth // LANES)]


START, EVEN, FIRST, LAST, PART, OFFSET, OTHERS = range(7)


def pack_kernel(copies, count, info, *refs):
    sources, outs, sems = refs[:count], refs[count:-1], refs[-1]
    started = []
    for number, (source, who, row, out, at) in enumerate(copies):
        begin = info[START] if who == 0 else info[OTHERS + who - 1]
        target = outs[out].at[at]
        rows = pl.ds(pl.multiple_of(begin + row, SUB), target.shape[1])
        copy = pltpu.make_async_copy(sources[source].at[:, rows, :], target, sems.at[number])
        copy.start()
        started.append(copy)
    for copy in started:
        copy.wait()


def slope_kernel(width, info, buoy, s1, s2, s3, scr):
    slab = scr.shape[0]
    pad_rows(scr, lambda row: buoy[:, aligned(info[START] + row), :] - 1.0, width)
    lane = lane_index(slab)

    def body(i, _):
        for h, cols in enumerate(columns(buoy.shape[2])):
            _, _, one, two, three = local_terms(scr, SUB * i, h, lane, False)
            s1[:, aligned(SUB * i), cols] = one
            s2[:, aligned(SUB * i), cols] = two
            s3[:, aligned(SUB * i), cols] = three
        return 0

    lax.fori_loop(0, width // SUB, body, 0)


def local_loop(width, start, depth, buoy, s2, s3, image, along, scr):
    lane = lane_index(scr.shape[0])

    def body(i, _):
        rows = aligned(SUB * i)
        for h, cols in enumerate(columns(depth)):
            _, lap, one, two, three = local_terms(scr, SUB * i, h, lane)
            b = buoy[:, aligned(start + SUB * i), cols]
            image[:, rows, cols] = b * lap + s2[:, rows, cols] * two + s3[:, rows, cols] * three
            along[:, rows, cols] = one
        return 0

    lax.fori_loop(0, width // SUB, body, 0)


def own_kernel(width, info, now, buoy, s2, s3, image, along, scr):
    pad_rows(scr, lambda row: now[:, aligned(info[START] + row), :], width)
    local_loop(width, info[START], now.shape[2], buoy, s2, s3, image, along, scr)


def far_kernel(width, split, info, now_a, now_b, buoy, s2, s3, image, along, whole, scr):
    halves = scr.shape[1]
    zero = jnp.zeros((scr.shape[0], SUB, LANES), jnp.float32)
    for h in range(halves):
        scr[:, h, pl.ds(0, SUB), :] = zero
        scr[:, h, pl.ds(width + SUB, SUB), :] = zero
    for ref, first in ((now_a, 0), (now_b, split)):

        def body(i, _):
            value = ref[0, :, aligned(SUB * i), :]
            whole[:, aligned(first + SUB * i), :] = value
            for h in range(halves):
                scr[:, h, aligned(first + SUB * (i + 1)), :] = value[:, :, h * LANES:(h + 1) * LANES]
            return 0

        lax.fori_loop(0, ref.shape[2] // SUB, body, 0)
    local_loop(width, info[START], buoy.shape[2], buoy, s2, s3, image, along, scr)


def planes_of(ref, index, rows, cols):
    return [ref[index, q, rows, cols] for q in range(REACH)]


def finish_kernel(parts, first_row, count, face_row, again, info, *refs):
    refs = list(refs)

    def take(n):
        got = refs[:n]
        del refs[:n]
        return got

    far = parts - 1
    in_own, out_own = take(2)
    ins, outs = take(far), take(far)
    now_own, before_own, pert_own, stiff, buoy, s1 = take(6)
    nows, pairs = take(far), take(far)
    images, alongs = take(parts), take(parts)
    earlier = take(2 + far) if again else ()
    following, slope, *scales, faces = refs
    start, base, offset = info[START], info[PART], info[OFFSET]
    first, last = info[FIRST] == 1, info[LAST] == 1
    slab, depth = s1.shape[0], s1.shape[2]

    def loop(even):
        def sides(index, inner, inner_rows, outer, outer_rows, cols):
            inside = planes_of(inner, index, inner_rows, cols)
            outside = planes_of(outer, index, outer_rows, cols)
            return (outside, inside) if even else (inside, outside)

        def body(i, _):
            part = aligned(SUB * i)
            rows = aligned(first_row + SUB * i)
            whole = aligned(start + first_row + SUB * i)
            for cols in columns(depth):
                low, high = sides(0, in_own, rows, out_own, part, cols)
                low = [jnp.where(first, 0.0, plane - 1.0) for plane in low]
                high = [jnp.where(last, 0.0, plane - 1.0) for plane in high]
                one = s1[:, rows, cols] + face_terms(low, high, slab, False)[1]
                slope[:, rows, cols] = one
                b, k = buoy[:, whole, cols], stiff[:, whole, cols]
                values = []
                for s in range(parts):
                    if s == 0:
                        low, high = sides(1, in_own, rows, out_own, part, cols)
                    else:
                        low, high = sides(0, ins[s - 1], part, outs[s - 1], part, cols)
                    lap, grad = face_terms(low, high, slab)
                    values.append(images[s][:, rows, cols] + b * lap + one * (alongs[s][:, rows, cols] + grad))
                source = values[0]
                for s in range(1, parts):
                    source = jnp.where(base == s, values[s], source)
                for s in range(parts):
                    if s == 0:
                        now, before = now_own[:, whole, cols], before_own[:, whole, cols]
                        scale = jnp.where(base == 0, 0.0, pert_own[:, whole, cols])
                    else:
                        now, before = nows[s - 1][:, rows, cols], pairs[s - 1][0, :, part, cols]
                        scale = jnp.where(base == s, 0.0, pairs[s - 1][1, :, part, cols])
                        scales[s - 1][:, rows, cols] = scale
                    following[s, :, rows, cols] = 2.0 * now - before + k * values[s] + scale * source
            return 0

        lax.fori_loop(0, count // SUB, body, 0)

    pl.when(info[EVEN] == 1)(lambda: loop(True))
    pl.when(info[EVEN] == 0)(lambda: loop(False))

    def keep(i, _):
        for source, target in zip(earlier, (following, slope, *scales)):
            rows = aligned(SUB * i)
            if len(source.shape) == 4:
                target[:, :, rows, :] = source[:, :, rows, :]
            else:
                target[:, rows, :] = source[:, rows, :]
        return 0

    if again:
        lax.fori_loop(0, first_row // SUB, keep, 0)

    def send(i, _):
        faces[:, :, aligned(SUB * i), :] = following[:, :, aligned(offset + face_row + SUB * i), :]
        return 0

    lax.fori_loop(0, faces.shape[2] // SUB, send, 0)


def start_kernel(parts, width, core, info, *refs):
    field, now_own, pert_own, stiff, buoy, s1, s2, s3 = refs[:8]
    nows, scales = refs[8:8 + parts - 1], refs[8 + parts - 1:8 + 2 * (parts - 1)]
    partial, scrs = refs[8 + 2 * (parts - 1)], refs[9 + 2 * (parts - 1):]
    start, base, offset = info[START], info[PART], info[OFFSET]
    for s in range(parts):
        pad_rows(scrs[s], lambda row, s=s: field[s, :, aligned(row), :], width)
    lane = lane_index(s1.shape[0])

    def body(i, _):
        out = aligned(SUB * i)
        rows = aligned(offset + SUB * i)
        whole = aligned(start + offset + SUB * i)
        for h, cols in enumerate(columns(s1.shape[2])):
            slopes = [ref[:, rows, cols] for ref in (s1, s2, s3)]
            b, k = buoy[:, whole, cols], stiff[:, whole, cols]
            centres, values = [], []
            for s in range(parts):
                centre, lap, one, two, three = local_terms(scrs[s], offset + SUB * i, h, lane)
                centres.append(centre)
                values.append(b * lap + slopes[0] * one + slopes[1] * two + slopes[2] * three)
            source = values[0]
            for s in range(1, parts):
                source = jnp.where(base == s, values[s], source)
            for s in range(parts):
                if s == 0:
                    now = now_own[:, whole, cols]
                    scale = jnp.where(base == 0, 0.0, pert_own[:, whole, cols])
                else:
                    now, scale = nows[s - 1][:, rows, cols], scales[s - 1][:, rows, cols]
                partial[s, :, out, cols] = 2.0 * centres[s] - now + k * values[s] + scale * source
        return 0

    lax.fori_loop(0, core // SUB, body, 0)


def end_kernel(parts, first_row, info, *refs):
    inner, outer, partial, pert_own, stiff, buoy, s1 = refs[:7]
    scales = refs[7:7 + parts - 1]
    own, others = refs[-2:]
    start, base, offset = info[START], info[PART], info[OFFSET]
    slab, depth, count = s1.shape[0], s1.shape[2], inner.shape[2]

    def loop(even):
        low_ref, high_ref = (outer, inner) if even else (inner, outer)

        def body(i, _):
            part = aligned(SUB * i)
            mine = aligned(first_row + SUB * i)
            rows = aligned(offset + first_row + SUB * i)
            whole = aligned(start + offset + first_row + SUB * i)
            for cols in columns(depth):
                b, k, one = buoy[:, whole, cols], stiff[:, whole, cols], s1[:, rows, cols]
                values = []
                for s in range(parts):
                    lap, grad = face_terms(
                        planes_of(low_ref, s, part, cols), planes_of(high_ref, s, part, cols), slab
                    )
                    values.append(b * lap + one * grad)
                source = values[0]
                for s in range(1, parts):
                    source = jnp.where(base == s, values[s], source)
                for s in range(parts):
                    if s == 0:
                        scale = jnp.where(base == 0, 0.0, pert_own[:, whole, cols])
                    else:
                        scale = scales[s - 1][:, rows, cols]
                    value = partial[s, :, mine, cols] + k * values[s] + scale * source
                    if s == 0:
                        own[:, part, cols] = value
                    else:
                        others[s - 1, :, part, cols] = value
            return 0

        lax.fori_loop(0, count // SUB, body, 0)

    pl.when(info[EVEN] == 1)(lambda: loop(True))
    pl.when(info[EVEN] == 0)(lambda: loop(False))


def call(kernel, info, args, outs, scratch=(), flops=0, space=None):
    vmem = pl.BlockSpec(memory_space=pltpu.VMEM)
    source = pl.BlockSpec(memory_space=space or pltpu.VMEM)
    outs = [jax.ShapeDtypeStruct(o, jnp.float32) for o in outs]
    size = flops = 1024 if TINY else sum(4 * a.size for a in args) + sum(4 * o.size for o in outs)
    return pl.pallas_call(
        kernel,
        name=kernel.func.__name__,
        out_shape=outs,
        in_specs=[pl.BlockSpec(memory_space=pltpu.SMEM)] + [source] * len(args),
        out_specs=[vmem] * len(outs),
        scratch_shapes=list(scratch),
        compiler_params=pltpu.CompilerParams(vmem_limit_bytes=12 << 20),
        cost_estimate=pl.CostEstimate(flops=flops, bytes_accessed=size, transcendentals=0),
    )(info, *args)


def lay_kernel(count, rows, *refs):
    pieces, result, sems = refs[:count], refs[-2], refs[-1]
    copies = []
    for number, piece in enumerate(pieces):
        target = result.at[:, pl.ds(pl.multiple_of(rows[number], SUB), piece.shape[1]), :]
        copy = pltpu.make_async_copy(piece, target, sems.at[number])
        copy.start()
        copies.append(copy)
    for copy in copies:
        copy.wait()


def lay(pieces, result, shape):
    rows = jnp.stack([row for row, _ in pieces]).astype(jnp.int32)
    pieces = [piece for _, piece in pieces]
    hbm = pl.BlockSpec(memory_space=pltpu.HBM)
    given = [] if result is None else [result]
    return pl.pallas_call(
        functools.partial(lay_kernel, len(pieces)),
        name="lay_kernel",
        out_shape=jax.ShapeDtypeStruct(shape, jnp.float32),
        in_specs=[pl.BlockSpec(memory_space=pltpu.SMEM)]
        + [pl.BlockSpec(memory_space=pltpu.VMEM)] * len(pieces)
        + [hbm] * len(given),
        out_specs=hbm,
        scratch_shapes=[pltpu.SemaphoreType.DMA((len(pieces),))],
        input_output_aliases={1 + len(pieces): 0} if given else {},
        compiler_params=pltpu.CompilerParams(vmem_limit_bytes=12 << 20),
    )(rows, *pieces, *given)


def after(value, *others):
    return lax.optimization_barrier((value, *others))[0]


def on_device(field_before, field_now, stiffness, buoyancy, perturbation):
    parts, count = lax.axis_size("probe"), lax.axis_size("space")
    part, place = lax.axis_index("probe"), lax.axis_index("space")
    before, now, pert = field_before[0], field_now[0], perturbation[0]
    slab, height, depth = now.shape
    far = parts - 1
    core = height // parts
    rim = 2 * REACH
    width = min(height, core + (2 if parts > 2 else 1) * rim)
    half = SUB * (core // SUB * HALF[0] // HALF[1])
    halves = (half, core - half)
    split = half + width - core
    chunks = (split, width - split)

    def window(p):
        return jnp.clip(core * p - rim, 0, height - width)

    even = place % 2 == 0
    info = jnp.stack(
        [window(part), even, place == 0, place == count - 1, part, core * part - window(part)]
        + [window((part + s) % parts) for s in range(1, parts)]
    ).astype(jnp.int32)

    inner_pairs = [(i, i ^ 1) for i in range(count)]
    outer_pairs = [(i, ((i + 1) ^ 1) - 1) for i in range(1, count - 1)]

    def swap(stack, pairs, from_end):
        if slab > REACH:
            stack = lax.dynamic_slice_in_dim(stack, jnp.where(from_end, slab - REACH, 0), REACH, axis=1)
        return lax.ppermute(stack, "space", pairs)

    def inside(stack):
        return swap(stack, inner_pairs, even)

    def outside(stack):
        return swap(stack, outer_pairs, jnp.logical_not(even))

    def turn(field, s):
        return lax.ppermute(field, "probe", [(i, (i + s) % parts) for i in range(parts)])

    def run_pack(args, copies, outs):
        return call(
            functools.partial(pack_kernel, tuple(copies), len(args)),
            info,
            args,
            outs,
            [pltpu.SemaphoreType.DMA((len(copies),))],
            space=pltpu.HBM,
        )

    spans = ((0, split), (split, width - split))
    copies, outs = [], []
    for span in ((0, width),) + spans:
        for f in range(2):
            copies.append((f, 0, span[0], len(outs), f))
        outs.append((2, slab, span[1], depth))
    for s in range(1, parts):
        for span in spans:
            copies.append((1, s, span[0], len(outs), 0))
            outs.append((1, slab, span[1], depth))
    face, face_a, face_b, *turning = run_pack(
        [pltpu.with_memory_space_constraint(field, pltpu.HBM) for field in (buoyancy, now)], copies, outs
    )

    out_own = [outside(face_a)]
    in_own = inside(face)
    nows = [[turn(turning[2 * (s - 1) + c], s) for s in range(1, parts)] for c in range(2)]
    out_own.append(outside(after(face_b, *nows[0])))

    scr = pltpu.VMEM((slab, depth // LANES, width + 2 * SUB, LANES), jnp.float32)
    wide = (slab, width, depth)
    cells = slab * width * depth
    s1, s2, s3 = call(functools.partial(slope_kernel, width), info, (after(buoyancy, in_own),), [wide] * 3, [scr], 33 * cells)

    copies, outs = [], []
    for s in range(1, parts):
        for span in spans:
            for f in range(2):
                copies.append((f, s, span[0], len(outs), f))
            outs.append((2, slab, span[1], depth))
    packed = run_pack((after(before, *nows[0]), pert), copies, outs)
    pairs = [[turn(packed[2 * (s - 1)], s) for s in range(1, parts)]]

    image, along = call(
        functools.partial(own_kernel, width), info, (now, buoyancy, s2, s3), [wide] * 2, [scr], 60 * cells
    )
    images, alongs = [image], [along]

    sent = nows[0]
    out_far = [[outside(field) for field in sent]]
    in_far = [[inside(field) for field in sent]]
    wholes = []
    for s in range(1, parts):
        image, along, whole = call(
            functools.partial(far_kernel, width, split),
            info,
            (nows[0][s - 1], nows[1][s - 1], buoyancy, s2, s3),
            [wide] * 3,
            [scr],
            60 * cells,
        )
        images.append(image)
        alongs.append(along)
        wholes.append(whole)
    sent = [after(field, images[-1]) for field in nows[1]]
    out_far.append([outside(field) for field in sent])
    in_far.append([inside(field) for field in sent])
    pairs.append([turn(after(packed[2 * (s - 1) + 1], images[-1]), s) for s in range(1, parts)])

    carried = ()
    faces = []
    for c in range(2):
        args = (
            [in_own, out_own[c]] + in_far[c] + out_far[c] + [now, before, pert, stiffness, buoyancy, s1]
            + wholes + pairs[c] + images + alongs
        )
        outs = [(parts, slab, width, depth), wide] + [wide] * far
        *carried, face = call(
            functools.partial(finish_kernel, parts, spans[c][0], spans[c][1], c * half, c == 1),
            info,
            (*args, *carried),
            outs + [(parts, slab, halves[c], depth)],
            (),
            45 * parts * spans[c][1] * slab * depth,
        )
        faces.append(face)
    following, slope, *scales = carried

    out_ends = [outside(face) for face in faces]
    in_ends = [inside(face) for face in faces]
    (partial,) = call(
        functools.partial(start_kernel, parts, width, core),
        info,
        (following, now, pert, stiffness, buoyancy, slope, s2, s3, *wholes, *scales),
        [(parts, slab, core, depth)],
        [scr] * parts,
        70 * parts * cells,
    )
    pieces = []
    for c in range(2):
        own, others = call(
            functools.partial(end_kernel, parts, c * half),
            info,
            (in_ends[c], out_ends[c], partial, pert, stiffness, buoyancy, slope, *scales),
            [(slab, halves[c], depth), (far, slab, halves[c], depth)],
            (),
            25 * parts * slab * halves[c] * depth,
        )
        pieces.append((core * part + c * half, own))
        for s in range(1, parts):
            row = core * ((part + s) % parts) + c * half
            pieces.append((row, turn(others[s - 1], parts - s)))
    result = lay(pieces[:-far], None, now.shape)
    result = lay(pieces[-far:], result, now.shape)
    return result[None]


def solution(mesh):
    placed = (
        P("probe", "space", None, None),
        P("probe", "space", None, None),
        P("space", None, None),
        P("space", None, None),
        P("probe", "space", None, None),
    )
    return jax.shard_map(
        on_device,
        mesh=mesh,
        in_specs=placed,
        out_specs=P("probe", "space", None, None),
        check_vma=False,
    )
```

```python
import functools

import jax
import jax.numpy as jnp
from jax import lax
from jax.experimental import pallas as pl
from jax.experimental.pallas import tpu as pltpu
from jax.sharding import PartitionSpec as P

STEPS = 2
REACH = 4
SUB = 8
LANES = 128
HALF = (1, 2)
TINY = True

second_coeffs = (8.0 / 5.0, -1.0 / 5.0, 8.0 / 315.0, -1.0 / 560.0)
first_coeffs = (4.0 / 5.0, -1.0 / 5.0, 4.0 / 105.0, -1.0 / 280.0)
centre_coeff = -205.0 / 72.0


def aligned(row):
    return pl.ds(pl.multiple_of(row, SUB), SUB)


def total_of(terms):
    total = None
    for term in terms:
        total = term if total is None else total + term
    return total


def pad_rows(scr, load, width):
    planes, halves = scr.shape[0], scr.shape[1]
    zero = jnp.zeros((planes, SUB, LANES), jnp.float32)
    for h in range(halves):
        scr[:, h, pl.ds(0, SUB), :] = zero
        scr[:, h, pl.ds(width + SUB, SUB), :] = zero

    def body(i, _):
        value = load(SUB * i)
        for h in range(halves):
            scr[:, h, aligned(SUB * (i + 1)), :] = value[:, :, h * LANES:(h + 1) * LANES]
        return 0

    lax.fori_loop(0, width // SUB, body, 0)


def local_terms(scr, row, h, lane, with_second=True):
    halves = scr.shape[1]
    here = [scr[:, j, aligned(row + SUB), :] for j in range(halves)]
    centre = here[h]
    slab = centre.shape[0]
    grads = ([], [])
    laps = []
    for k in range(1, REACH + 1):
        up = pltpu.roll(centre, LANES - k, 2)
        down = pltpu.roll(centre, k, 2)
        above = pltpu.roll(here[h + 1], LANES - k, 2) if h + 1 < halves else 0.0
        below = pltpu.roll(here[h - 1], k, 2) if h > 0 else 0.0
        up = jnp.where(lane < LANES - k, up, above)
        down = jnp.where(lane >= k, down, below)
        right = scr[:, h, pl.ds(row + SUB + k, SUB), :]
        left = scr[:, h, pl.ds(row + SUB - k, SUB), :]
        grads[0].append(first_coeffs[k - 1] * (right - left))
        grads[1].append(first_coeffs[k - 1] * (up - down))
        if with_second:
            laps.append(second_coeffs[k - 1] * ((right + left) + (up + down)))
    planes = []
    plane_laps = []
    for p in range(slab):
        first, second = [], []
        for k in range(1, REACH + 1):
            high = centre[p + k] if p + k < slab else None
            low = centre[p - k] if p >= k else None
            if high is not None and low is not None:
                first.append(first_coeffs[k - 1] * (high - low))
                second.append(second_coeffs[k - 1] * (high + low))
            elif high is not None:
                first.append(first_coeffs[k - 1] * high)
                second.append(second_coeffs[k - 1] * high)
            elif low is not None:
                first.append(-first_coeffs[k - 1] * low)
                second.append(second_coeffs[k - 1] * low)
        planes.append(total_of(first))
        plane_laps.append(total_of(second))
    along = jnp.stack(planes)
    lap = None
    if with_second:
        lap = total_of(laps + [(3.0 * centre_coeff) * centre, jnp.stack(plane_laps)])
    return centre, lap, along, total_of(grads[0]), total_of(grads[1])


def face_terms(low, high, slab, with_second=True):
    laps, grads = [], []
    for p in range(slab):
        first, second = [], []
        for k in range(1, REACH + 1):
            if p + k >= slab:
                plane = high[p + k - slab]
                first.append(first_coeffs[k - 1] * plane)
                second.append(second_coeffs[k - 1] * plane)
            if p - k < 0:
                plane = low[REACH + p - k]
                first.append(-first_coeffs[k - 1] * plane)
                second.append(second_coeffs[k - 1] * plane)
        zero = jnp.zeros_like(low[0])
        grads.append(total_of(first) if first else zero)
        laps.append(total_of(second) if second else zero)
    return (jnp.stack(laps) if with_second else None), jnp.stack(grads)


def lane_index(slab):
    return lax.broadcasted_iota(jnp.int32, (slab, SUB, LANES), 2)


def columns(depth):
    return [slice(h * LANES, (h + 1) * LANES) for h in range(depth // LANES)]


START, EVEN, FIRST, LAST, PART, OFFSET, OTHERS = range(7)


def pack_kernel(copies, count, info, *refs):
    sources, outs, sems = refs[:count], refs[count:-1], refs[-1]
    started = []
    for number, (source, who, row, out, at) in enumerate(copies):
        begin = info[START] if who == 0 else info[OTHERS + who - 1]
        target = outs[out].at[at]
        rows = pl.ds(pl.multiple_of(begin + row, SUB), target.shape[1])
        copy = pltpu.make_async_copy(sources[source].at[:, rows, :], target, sems.at[number])
        copy.start()
        started.append(copy)
    for copy in started:
        copy.wait()


def slope_kernel(width, info, buoy, s1, s2, s3, scr):
    slab = scr.shape[0]
    pad_rows(scr, lambda row: buoy[:, aligned(info[START] + row), :] - 1.0, width)
    lane = lane_index(slab)

    def body(i, _):
        for h, cols in enumerate(columns(buoy.shape[2])):
            _, _, one, two, three = local_terms(scr, SUB * i, h, lane, False)
            s1[:, aligned(SUB * i), cols] = one
            s2[:, aligned(SUB * i), cols] = two
            s3[:, aligned(SUB * i), cols] = three
        return 0

    lax.fori_loop(0, width // SUB, body, 0)


def local_loop(width, start, depth, buoy, s2, s3, image, along, scr):
    lane = lane_index(scr.shape[0])

    def body(i, _):
        rows = aligned(SUB * i)
        for h, cols in enumerate(columns(depth)):
            _, lap, one, two, three = local_terms(scr, SUB * i, h, lane)
            b = buoy[:, aligned(start + SUB * i), cols]
            image[:, rows, cols] = b * lap + s2[:, rows, cols] * two + s3[:, rows, cols] * three
            along[:, rows, cols] = one
        return 0

    lax.fori_loop(0, width // SUB, body, 0)


def own_kernel(width, info, now, buoy, s2, s3, image, along, scr):
    pad_rows(scr, lambda row: now[:, aligned(info[START] + row), :], width)
    local_loop(width, info[START], now.shape[2], buoy, s2, s3, image, along, scr)


def far_kernel(width, split, info, now_a, now_b, buoy, s2, s3, image, along, whole, scr):
    halves = scr.shape[1]
    zero = jnp.zeros((scr.shape[0], SUB, LANES), jnp.float32)
    for h in range(halves):
        scr[:, h, pl.ds(0, SUB), :] = zero
        scr[:, h, pl.ds(width + SUB, SUB), :] = zero
    for ref, first in ((now_a, 0), (now_b, split)):

        def body(i, _):
            value = ref[0, :, aligned(SUB * i), :]
            whole[:, aligned(first + SUB * i), :] = value
            for h in range(halves):
                scr[:, h, aligned(first + SUB * (i + 1)), :] = value[:, :, h * LANES:(h + 1) * LANES]
            return 0

        lax.fori_loop(0, ref.shape[2] // SUB, body, 0)
    local_loop(width, info[START], buoy.shape[2], buoy, s2, s3, image, along, scr)


def planes_of(ref, index, rows, cols):
    return [ref[index, q, rows, cols] for q in range(REACH)]


def finish_kernel(parts, first_row, count, face_row, again, info, *refs):
    refs = list(refs)

    def take(n):
        got = refs[:n]
        del refs[:n]
        return got

    far = parts - 1
    in_own, out_own = take(2)
    ins, outs = take(far), take(far)
    now_own, before_own, pert_own, stiff, buoy, s1 = take(6)
    nows, pairs = take(far), take(far)
    images, alongs = take(parts), take(parts)
    earlier = take(2 + far) if again else ()
    following, slope, *scales, faces = refs
    start, base, offset = info[START], info[PART], info[OFFSET]
    first, last = info[FIRST] == 1, info[LAST] == 1
    slab, depth = s1.shape[0], s1.shape[2]

    def loop(even):
        def sides(index, inner, inner_rows, outer, outer_rows, cols):
            inside = planes_of(inner, index, inner_rows, cols)
            outside = planes_of(outer, index, outer_rows, cols)
            return (outside, inside) if even else (inside, outside)

        def body(i, _):
            part = aligned(SUB * i)
            rows = aligned(first_row + SUB * i)
            whole = aligned(start + first_row + SUB * i)
            for cols in columns(depth):
                low, high = sides(0, in_own, rows, out_own, part, cols)
                low = [jnp.where(first, 0.0, plane - 1.0) for plane in low]
                high = [jnp.where(last, 0.0, plane - 1.0) for plane in high]
                one = s1[:, rows, cols] + face_terms(low, high, slab, False)[1]
                slope[:, rows, cols] = one
                b, k = buoy[:, whole, cols], stiff[:, whole, cols]
                values = []
                for s in range(parts):
                    if s == 0:
                        low, high = sides(1, in_own, rows, out_own, part, cols)
                    else:
                        low, high = sides(0, ins[s - 1], part, outs[s - 1], part, cols)
                    lap, grad = face_terms(low, high, slab)
                    values.append(images[s][:, rows, cols] + b * lap + one * (alongs[s][:, rows, cols] + grad))
                source = values[0]
                for s in range(1, parts):
                    source = jnp.where(base == s, values[s], source)
                for s in range(parts):
                    if s == 0:
                        now, before = now_own[:, whole, cols], before_own[:, whole, cols]
                        scale = jnp.where(base == 0, 0.0, pert_own[:, whole, cols])
                    else:
                        now, before = nows[s - 1][:, rows, cols], pairs[s - 1][0, :, part, cols]
                        scale = jnp.where(base == s, 0.0, pairs[s - 1][1, :, part, cols])
                        scales[s - 1][:, rows, cols] = scale
                    following[s, :, rows, cols] = 2.0 * now - before + k * values[s] + scale * source
            return 0

        lax.fori_loop(0, count // SUB, body, 0)

    pl.when(info[EVEN] == 1)(lambda: loop(True))
    pl.when(info[EVEN] == 0)(lambda: loop(False))

    def keep(i, _):
        for source, target in zip(earlier, (following, slope, *scales)):
            rows = aligned(SUB * i)
            if len(source.shape) == 4:
                target[:, :, rows, :] = source[:, :, rows, :]
            else:
                target[:, rows, :] = source[:, rows, :]
        return 0

    if again:
        lax.fori_loop(0, first_row // SUB, keep, 0)

    def send(i, _):
        faces[:, :, aligned(SUB * i), :] = following[:, :, aligned(offset + face_row + SUB * i), :]
        return 0

    lax.fori_loop(0, faces.shape[2] // SUB, send, 0)


def start_kernel(parts, width, core, info, *refs):
    field, now_own, pert_own, stiff, buoy, s1, s2, s3 = refs[:8]
    nows, scales = refs[8:8 + parts - 1], refs[8 + parts - 1:8 + 2 * (parts - 1)]
    partial, scrs = refs[8 + 2 * (parts - 1)], refs[9 + 2 * (parts - 1):]
    start, base, offset = info[START], info[PART], info[OFFSET]
    for s in range(parts):
        pad_rows(scrs[s], lambda row, s=s: field[s, :, aligned(row), :], width)
    lane = lane_index(s1.shape[0])

    def body(i, _):
        out = aligned(SUB * i)
        rows = aligned(offset + SUB * i)
        whole = aligned(start + offset + SUB * i)
        for h, cols in enumerate(columns(s1.shape[2])):
            slopes = [ref[:, rows, cols] for ref in (s1, s2, s3)]
            b, k = buoy[:, whole, cols], stiff[:, whole, cols]
            centres, values = [], []
            for s in range(parts):
                centre, lap, one, two, three = local_terms(scrs[s], offset + SUB * i, h, lane)
                centres.append(centre)
                values.append(b * lap + slopes[0] * one + slopes[1] * two + slopes[2] * three)
            source = values[0]
            for s in range(1, parts):
                source = jnp.where(base == s, values[s], source)
            for s in range(parts):
                if s == 0:
                    now = now_own[:, whole, cols]
                    scale = jnp.where(base == 0, 0.0, pert_own[:, whole, cols])
                else:
                    now, scale = nows[s - 1][:, rows, cols], scales[s - 1][:, rows, cols]
                partial[s, :, out, cols] = 2.0 * centres[s] - now + k * values[s] + scale * source
        return 0

    lax.fori_loop(0, core // SUB, body, 0)


def end_kernel(parts, first_row, info, *refs):
    inner, outer, partial, pert_own, stiff, buoy, s1 = refs[:7]
    scales = refs[7:7 + parts - 1]
    own, others = refs[-2:]
    start, base, offset = info[START], info[PART], info[OFFSET]
    slab, depth, count = s1.shape[0], s1.shape[2], inner.shape[2]

    def loop(even):
        low_ref, high_ref = (outer, inner) if even else (inner, outer)

        def body(i, _):
            part = aligned(SUB * i)
            mine = aligned(first_row + SUB * i)
            rows = aligned(offset + first_row + SUB * i)
            whole = aligned(start + offset + first_row + SUB * i)
            for cols in columns(depth):
                b, k, one = buoy[:, whole, cols], stiff[:, whole, cols], s1[:, rows, cols]
                values = []
                for s in range(parts):
                    lap, grad = face_terms(
                        planes_of(low_ref, s, part, cols), planes_of(high_ref, s, part, cols), slab
                    )
                    values.append(b * lap + one * grad)
                source = values[0]
                for s in range(1, parts):
                    source = jnp.where(base == s, values[s], source)
                for s in range(parts):
                    if s == 0:
                        scale = jnp.where(base == 0, 0.0, pert_own[:, whole, cols])
                    else:
                        scale = scales[s - 1][:, rows, cols]
                    value = partial[s, :, mine, cols] + k * values[s] + scale * source
                    if s == 0:
                        own[:, part, cols] = value
                    else:
                        others[s - 1, :, part, cols] = value
            return 0

        lax.fori_loop(0, count // SUB, body, 0)

    pl.when(info[EVEN] == 1)(lambda: loop(True))
    pl.when(info[EVEN] == 0)(lambda: loop(False))


def call(kernel, info, args, outs, scratch=(), flops=0, space=None):
    vmem = pl.BlockSpec(memory_space=pltpu.VMEM)
    source = pl.BlockSpec(memory_space=space or pltpu.VMEM)
    outs = [jax.ShapeDtypeStruct(o, jnp.float32) for o in outs]
    size = flops = 1024 if TINY else sum(4 * a.size for a in args) + sum(4 * o.size for o in outs)
    return pl.pallas_call(
        kernel,
        name=kernel.func.__name__,
        out_shape=outs,
        in_specs=[pl.BlockSpec(memory_space=pltpu.SMEM)] + [source] * len(args),
        out_specs=[vmem] * len(outs),
        scratch_shapes=list(scratch),
        compiler_params=pltpu.CompilerParams(vmem_limit_bytes=12 << 20),
        cost_estimate=pl.CostEstimate(flops=flops, bytes_accessed=size, transcendentals=0),
    )(info, *args)


def lay_kernel(count, rows, *refs):
    pieces, result, sems = refs[:count], refs[-2], refs[-1]
    copies = []
    for number, piece in enumerate(pieces):
        target = result.at[:, pl.ds(pl.multiple_of(rows[number], SUB), piece.shape[1]), :]
        copy = pltpu.make_async_copy(piece, target, sems.at[number])
        copy.start()
        copies.append(copy)
    for copy in copies:
        copy.wait()


def lay(pieces, result, shape):
    rows = jnp.stack([row for row, _ in pieces]).astype(jnp.int32)
    pieces = [piece for _, piece in pieces]
    hbm = pl.BlockSpec(memory_space=pltpu.HBM)
    given = [] if result is None else [result]
    return pl.pallas_call(
        functools.partial(lay_kernel, len(pieces)),
        name="lay_kernel",
        out_shape=jax.ShapeDtypeStruct(shape, jnp.float32),
        in_specs=[pl.BlockSpec(memory_space=pltpu.SMEM)]
        + [pl.BlockSpec(memory_space=pltpu.VMEM)] * len(pieces)
        + [hbm] * len(given),
        out_specs=hbm,
        scratch_shapes=[pltpu.SemaphoreType.DMA((len(pieces),))],
        input_output_aliases={1 + len(pieces): 0} if given else {},
        compiler_params=pltpu.CompilerParams(vmem_limit_bytes=12 << 20),
    )(rows, *pieces, *given)


def after(value, *others):
    return lax.optimization_barrier((value, *others))[0]


def on_device(field_before, field_now, stiffness, buoyancy, perturbation):
    parts, count = lax.axis_size("probe"), lax.axis_size("space")
    part, place = lax.axis_index("probe"), lax.axis_index("space")
    before, now, pert = field_before[0], field_now[0], perturbation[0]
    slab, height, depth = now.shape
    far = parts - 1
    core = height // parts
    rim = 2 * REACH
    width = min(height, core + (2 if parts > 2 else 1) * rim)
    half = SUB * (core // SUB * HALF[0] // HALF[1])
    halves = (half, core - half)
    split = half + width - core
    chunks = (split, width - split)

    def window(p):
        return jnp.clip(core * p - rim, 0, height - width)

    even = place % 2 == 0
    info = jnp.stack(
        [window(part), even, place == 0, place == count - 1, part, core * part - window(part)]
        + [window((part + s) % parts) for s in range(1, parts)]
    ).astype(jnp.int32)

    inner_pairs = [(i, i ^ 1) for i in range(count)]
    outer_pairs = [(i, ((i + 1) ^ 1) - 1) for i in range(1, count - 1)]

    def swap(stack, pairs, from_end):
        if slab > REACH:
            stack = lax.dynamic_slice_in_dim(stack, jnp.where(from_end, slab - REACH, 0), REACH, axis=1)
        return lax.ppermute(stack, "space", pairs)

    def inside(stack):
        return swap(stack, inner_pairs, even)

    def outside(stack):
        return swap(stack, outer_pairs, jnp.logical_not(even))

    def turn(field, s):
        return lax.ppermute(field, "probe", [(i, (i + s) % parts) for i in range(parts)])

    def run_pack(args, copies, outs):
        return call(
            functools.partial(pack_kernel, tuple(copies), len(args)),
            info,
            args,
            outs,
            [pltpu.SemaphoreType.DMA((len(copies),))],
            space=pltpu.HBM,
        )

    spans = ((0, split), (split, width - split))
    copies, outs = [], []
    for span in ((0, width),) + spans:
        for f in range(2):
            copies.append((f, 0, span[0], len(outs), f))
        outs.append((2, slab, span[1], depth))
    for s in range(1, parts):
        for span in spans:
            copies.append((1, s, span[0], len(outs), 0))
            outs.append((1, slab, span[1], depth))
    face, face_a, face_b, *turning = run_pack(
        [pltpu.with_memory_space_constraint(field, pltpu.HBM) for field in (buoyancy, now)], copies, outs
    )

    out_own = [outside(face_a)]
    in_own = inside(face)
    nows = [[turn(turning[2 * (s - 1)], s) for s in range(1, parts)]]
    out_far = [[outside(field) for field in nows[0]]]
    in_far = [[inside(field) for field in nows[0]]]
    nows.append([turn(after(turning[2 * s - 1], *in_far[0]), s) for s in range(1, parts)])
    out_own.append(outside(after(face_b, *nows[0])))

    scr = pltpu.VMEM((slab, depth // LANES, width + 2 * SUB, LANES), jnp.float32)
    wide = (slab, width, depth)
    cells = slab * width * depth
    s1, s2, s3 = call(functools.partial(slope_kernel, width), info, (after(buoyancy, in_own, out_own[0]),), [wide] * 3, [scr], 33 * cells)

    copies, outs = [], []
    for s in range(1, parts):
        for span in spans:
            for f in range(2):
                copies.append((f, s, span[0], len(outs), f))
            outs.append((2, slab, span[1], depth))
    packed = run_pack((after(before, *nows[0]), pert), copies, outs)
    pairs = [[turn(packed[2 * (s - 1)], s) for s in range(1, parts)]]

    image, along = call(
        functools.partial(own_kernel, width), info, (now, buoyancy, s2, s3), [wide] * 2, [scr], 60 * cells
    )
    images, alongs = [image], [along]

    wholes = []
    for s in range(1, parts):
        image, along, whole = call(
            functools.partial(far_kernel, width, split),
            info,
            (nows[0][s - 1], nows[1][s - 1], buoyancy, s2, s3),
            [wide] * 3,
            [scr],
            60 * cells,
        )
        images.append(image)
        alongs.append(along)
        wholes.append(whole)
    sent = [after(field, images[-1]) for field in nows[1]]
    out_far.append([outside(field) for field in sent])
    in_far.append([inside(field) for field in sent])
    pairs.append([turn(after(packed[2 * (s - 1) + 1], images[-1]), s) for s in range(1, parts)])

    carried = ()
    faces = []
    for c in range(2):
        args = (
            [in_own, out_own[c]] + in_far[c] + out_far[c] + [now, before, pert, stiffness, buoyancy, s1]
            + wholes + pairs[c] + images + alongs
        )
        outs = [(parts, slab, width, depth), wide] + [wide] * far
        *carried, face = call(
            functools.partial(finish_kernel, parts, spans[c][0], spans[c][1], c * half, c == 1),
            info,
            (*args, *carried),
            outs + [(parts, slab, halves[c], depth)],
            (),
            45 * parts * spans[c][1] * slab * depth,
        )
        faces.append(face)
    following, slope, *scales = carried

    out_ends = [outside(face) for face in faces]
    in_ends = [inside(face) for face in faces]
    (partial,) = call(
        functools.partial(start_kernel, parts, width, core),
        info,
        (following, now, pert, stiffness, buoyancy, slope, s2, s3, *wholes, *scales),
        [(parts, slab, core, depth)],
        [scr] * parts,
        70 * parts * cells,
    )
    pieces = []
    for c in range(2):
        own, others = call(
            functools.partial(end_kernel, parts, c * half),
            info,
            (in_ends[c], out_ends[c], partial, pert, stiffness, buoyancy, slope, *scales),
            [(slab, halves[c], depth), (far, slab, halves[c], depth)],
            (),
            25 * parts * slab * halves[c] * depth,
        )
        pieces.append((core * part + c * half, own))
        for s in range(1, parts):
            row = core * ((part + s) % parts) + c * half
            pieces.append((row, turn(others[s - 1], parts - s)))
    result = lay(pieces[:-far], None, now.shape)
    result = lay(pieces[-far:], result, now.shape)
    return result[None]


def solution(mesh):
    placed = (
        P("probe", "space", None, None),
        P("probe", "space", None, None),
        P("space", None, None),
        P("space", None, None),
        P("probe", "space", None, None),
    )
    return jax.shard_map(
        on_device,
        mesh=mesh,
        in_specs=placed,
        out_specs=P("probe", "space", None, None),
        check_vma=False,
    )
```

```python
import functools

import jax
import jax.numpy as jnp
from jax import lax
from jax.experimental import pallas as pl
from jax.experimental.pallas import tpu as pltpu
from jax.sharding import PartitionSpec as P

STEPS = 2
REACH = 4
SUB = 8
LANES = 128
HALF = (1, 2)
TINY = True

second_coeffs = (8.0 / 5.0, -1.0 / 5.0, 8.0 / 315.0, -1.0 / 560.0)
first_coeffs = (4.0 / 5.0, -1.0 / 5.0, 4.0 / 105.0, -1.0 / 280.0)
centre_coeff = -205.0 / 72.0


def aligned(row):
    return pl.ds(pl.multiple_of(row, SUB), SUB)


def total_of(terms):
    total = None
    for term in terms:
        total = term if total is None else total + term
    return total


def pad_rows(scr, load, width):
    planes, halves = scr.shape[0], scr.shape[1]
    zero = jnp.zeros((planes, SUB, LANES), jnp.float32)
    for h in range(halves):
        scr[:, h, pl.ds(0, SUB), :] = zero
        scr[:, h, pl.ds(width + SUB, SUB), :] = zero

    def body(i, _):
        value = load(SUB * i)
        for h in range(halves):
            scr[:, h, aligned(SUB * (i + 1)), :] = value[:, :, h * LANES:(h + 1) * LANES]
        return 0

    lax.fori_loop(0, width // SUB, body, 0)


def local_terms(scr, row, h, lane, with_second=True):
    halves = scr.shape[1]
    here = [scr[:, j, aligned(row + SUB), :] for j in range(halves)]
    centre = here[h]
    slab = centre.shape[0]
    grads = ([], [])
    laps = []
    for k in range(1, REACH + 1):
        up = pltpu.roll(centre, LANES - k, 2)
        down = pltpu.roll(centre, k, 2)
        above = pltpu.roll(here[h + 1], LANES - k, 2) if h + 1 < halves else 0.0
        below = pltpu.roll(here[h - 1], k, 2) if h > 0 else 0.0
        up = jnp.where(lane < LANES - k, up, above)
        down = jnp.where(lane >= k, down, below)
        right = scr[:, h, pl.ds(row + SUB + k, SUB), :]
        left = scr[:, h, pl.ds(row + SUB - k, SUB), :]
        grads[0].append(first_coeffs[k - 1] * (right - left))
        grads[1].append(first_coeffs[k - 1] * (up - down))
        if with_second:
            laps.append(second_coeffs[k - 1] * ((right + left) + (up + down)))
    planes = []
    plane_laps = []
    for p in range(slab):
        first, second = [], []
        for k in range(1, REACH + 1):
            high = centre[p + k] if p + k < slab else None
            low = centre[p - k] if p >= k else None
            if high is not None and low is not None:
                first.append(first_coeffs[k - 1] * (high - low))
                second.append(second_coeffs[k - 1] * (high + low))
            elif high is not None:
                first.append(first_coeffs[k - 1] * high)
                second.append(second_coeffs[k - 1] * high)
            elif low is not None:
                first.append(-first_coeffs[k - 1] * low)
                second.append(second_coeffs[k - 1] * low)
        planes.append(total_of(first))
        plane_laps.append(total_of(second))
    along = jnp.stack(planes)
    lap = None
    if with_second:
        lap = total_of(laps + [(3.0 * centre_coeff) * centre, jnp.stack(plane_laps)])
    return centre, lap, along, total_of(grads[0]), total_of(grads[1])


def face_terms(low, high, slab, with_second=True):
    laps, grads = [], []
    for p in range(slab):
        first, second = [], []
        for k in range(1, REACH + 1):
            if p + k >= slab:
                plane = high[p + k - slab]
                first.append(first_coeffs[k - 1] * plane)
                second.append(second_coeffs[k - 1] * plane)
            if p - k < 0:
                plane = low[REACH + p - k]
                first.append(-first_coeffs[k - 1] * plane)
                second.append(second_coeffs[k - 1] * plane)
        zero = jnp.zeros_like(low[0])
        grads.append(total_of(first) if first else zero)
        laps.append(total_of(second) if second else zero)
    return (jnp.stack(laps) if with_second else None), jnp.stack(grads)


def lane_index(slab):
    return lax.broadcasted_iota(jnp.int32, (slab, SUB, LANES), 2)


def columns(depth):
    return [slice(h * LANES, (h + 1) * LANES) for h in range(depth // LANES)]


START, EVEN, FIRST, LAST, PART, OFFSET, OTHERS = range(7)


def pack_kernel(copies, count, info, *refs):
    sources, outs, sems = refs[:count], refs[count:-1], refs[-1]
    started = []
    for number, (source, who, row, out, at) in enumerate(copies):
        begin = info[START] if who == 0 else info[OTHERS + who - 1]
        target = outs[out].at[at]
        rows = pl.ds(pl.multiple_of(begin + row, SUB), target.shape[1])
        copy = pltpu.make_async_copy(sources[source].at[:, rows, :], target, sems.at[number])
        copy.start()
        started.append(copy)
    for copy in started:
        copy.wait()


def slope_kernel(width, info, buoy, s1, s2, s3, scr):
    slab = scr.shape[0]
    pad_rows(scr, lambda row: buoy[:, aligned(info[START] + row), :] - 1.0, width)
    lane = lane_index(slab)

    def body(i, _):
        for h, cols in enumerate(columns(buoy.shape[2])):
            _, _, one, two, three = local_terms(scr, SUB * i, h, lane, False)
            s1[:, aligned(SUB * i), cols] = one
            s2[:, aligned(SUB * i), cols] = two
            s3[:, aligned(SUB * i), cols] = three
        return 0

    lax.fori_loop(0, width // SUB, body, 0)


def local_loop(width, start, depth, buoy, s2, s3, image, along, scr):
    lane = lane_index(scr.shape[0])

    def body(i, _):
        rows = aligned(SUB * i)
        for h, cols in enumerate(columns(depth)):
            _, lap, one, two, three = local_terms(scr, SUB * i, h, lane)
            b = buoy[:, aligned(start + SUB * i), cols]
            image[:, rows, cols] = b * lap + s2[:, rows, cols] * two + s3[:, rows, cols] * three
            along[:, rows, cols] = one
        return 0

    lax.fori_loop(0, width // SUB, body, 0)


def own_kernel(width, info, now, buoy, s2, s3, image, along, scr):
    pad_rows(scr, lambda row: now[:, aligned(info[START] + row), :], width)
    local_loop(width, info[START], now.shape[2], buoy, s2, s3, image, along, scr)


def far_kernel(width, split, info, now_a, now_b, buoy, s2, s3, image, along, whole, scr):
    halves = scr.shape[1]
    zero = jnp.zeros((scr.shape[0], SUB, LANES), jnp.float32)
    for h in range(halves):
        scr[:, h, pl.ds(0, SUB), :] = zero
        scr[:, h, pl.ds(width + SUB, SUB), :] = zero
    for ref, first in ((now_a, 0), (now_b, split)):

        def body(i, _):
            value = ref[0, :, aligned(SUB * i), :]
            whole[:, aligned(first + SUB * i), :] = value
            for h in range(halves):
                scr[:, h, aligned(first + SUB * (i + 1)), :] = value[:, :, h * LANES:(h + 1) * LANES]
            return 0

        lax.fori_loop(0, ref.shape[2] // SUB, body, 0)
    local_loop(width, info[START], buoy.shape[2], buoy, s2, s3, image, along, scr)


def planes_of(ref, index, rows, cols):
    return [ref[index, q, rows, cols] for q in range(REACH)]


def finish_kernel(parts, first_row, count, face_row, again, info, *refs):
    refs = list(refs)

    def take(n):
        got = refs[:n]
        del refs[:n]
        return got

    far = parts - 1
    in_own, out_own = take(2)
    ins, outs = take(far), take(far)
    now_own, before_own, pert_own, stiff, buoy, s1 = take(6)
    nows, pairs = take(far), take(far)
    images, alongs = take(parts), take(parts)
    earlier = take(2 + far) if again else ()
    following, slope, *scales, faces = refs
    start, base, offset = info[START], info[PART], info[OFFSET]
    first, last = info[FIRST] == 1, info[LAST] == 1
    slab, depth = s1.shape[0], s1.shape[2]

    def loop(even):
        def sides(index, inner, inner_rows, outer, outer_rows, cols):
            inside = planes_of(inner, index, inner_rows, cols)
            outside = planes_of(outer, index, outer_rows, cols)
            return (outside, inside) if even else (inside, outside)

        def body(i, _):
            part = aligned(SUB * i)
            rows = aligned(first_row + SUB * i)
            whole = aligned(start + first_row + SUB * i)
            for cols in columns(depth):
                low, high = sides(0, in_own, rows, out_own, part, cols)
                low = [jnp.where(first, 0.0, plane - 1.0) for plane in low]
                high = [jnp.where(last, 0.0, plane - 1.0) for plane in high]
                one = s1[:, rows, cols] + face_terms(low, high, slab, False)[1]
                slope[:, rows, cols] = one
                b, k = buoy[:, whole, cols], stiff[:, whole, cols]
                values = []
                for s in range(parts):
                    if s == 0:
                        low, high = sides(1, in_own, rows, out_own, part, cols)
                    else:
                        low, high = sides(0, ins[s - 1], part, outs[s - 1], part, cols)
                    lap, grad = face_terms(low, high, slab)
                    values.append(images[s][:, rows, cols] + b * lap + one * (alongs[s][:, rows, cols] + grad))
                source = values[0]
                for s in range(1, parts):
                    source = jnp.where(base == s, values[s], source)
                for s in range(parts):
                    if s == 0:
                        now, before = now_own[:, whole, cols], before_own[:, whole, cols]
                        scale = jnp.where(base == 0, 0.0, pert_own[:, whole, cols])
                    else:
                        now, before = nows[s - 1][:, rows, cols], pairs[s - 1][0, :, part, cols]
                        scale = jnp.where(base == s, 0.0, pairs[s - 1][1, :, part, cols])
                        scales[s - 1][:, rows, cols] = scale
                    following[s, :, rows, cols] = 2.0 * now - before + k * values[s] + scale * source
            return 0

        lax.fori_loop(0, count // SUB, body, 0, unroll=2)

    pl.when(info[EVEN] == 1)(lambda: loop(True))
    pl.when(info[EVEN] == 0)(lambda: loop(False))

    def keep(i, _):
        for source, target in zip(earlier, (following, slope, *scales)):
            rows = aligned(SUB * i)
            if len(source.shape) == 4:
                target[:, :, rows, :] = source[:, :, rows, :]
            else:
                target[:, rows, :] = source[:, rows, :]
        return 0

    if again:
        lax.fori_loop(0, first_row // SUB, keep, 0)

    def send(i, _):
        faces[:, :, aligned(SUB * i), :] = following[:, :, aligned(offset + face_row + SUB * i), :]
        return 0

    lax.fori_loop(0, faces.shape[2] // SUB, send, 0)


def start_kernel(parts, width, core, info, *refs):
    field, now_own, pert_own, stiff, buoy, s1, s2, s3 = refs[:8]
    nows, scales = refs[8:8 + parts - 1], refs[8 + parts - 1:8 + 2 * (parts - 1)]
    partial, scrs = refs[8 + 2 * (parts - 1)], refs[9 + 2 * (parts - 1):]
    start, base, offset = info[START], info[PART], info[OFFSET]
    for s in range(parts):
        pad_rows(scrs[s], lambda row, s=s: field[s, :, aligned(row), :], width)
    lane = lane_index(s1.shape[0])

    def body(i, _):
        out = aligned(SUB * i)
        rows = aligned(offset + SUB * i)
        whole = aligned(start + offset + SUB * i)
        for h, cols in enumerate(columns(s1.shape[2])):
            slopes = [ref[:, rows, cols] for ref in (s1, s2, s3)]
            b, k = buoy[:, whole, cols], stiff[:, whole, cols]
            centres, values = [], []
            for s in range(parts):
                centre, lap, one, two, three = local_terms(scrs[s], offset + SUB * i, h, lane)
                centres.append(centre)
                values.append(b * lap + slopes[0] * one + slopes[1] * two + slopes[2] * three)
            source = values[0]
            for s in range(1, parts):
                source = jnp.where(base == s, values[s], source)
            for s in range(parts):
                if s == 0:
                    now = now_own[:, whole, cols]
                    scale = jnp.where(base == 0, 0.0, pert_own[:, whole, cols])
                else:
                    now, scale = nows[s - 1][:, rows, cols], scales[s - 1][:, rows, cols]
                partial[s, :, out, cols] = 2.0 * centres[s] - now + k * values[s] + scale * source
        return 0

    lax.fori_loop(0, core // SUB, body, 0)


def end_kernel(parts, first_row, info, *refs):
    inner, outer, partial, pert_own, stiff, buoy, s1 = refs[:7]
    scales = refs[7:7 + parts - 1]
    own, others = refs[-2:]
    start, base, offset = info[START], info[PART], info[OFFSET]
    slab, depth, count = s1.shape[0], s1.shape[2], inner.shape[2]

    def loop(even):
        low_ref, high_ref = (outer, inner) if even else (inner, outer)

        def body(i, _):
            part = aligned(SUB * i)
            mine = aligned(first_row + SUB * i)
            rows = aligned(offset + first_row + SUB * i)
            whole = aligned(start + offset + first_row + SUB * i)
            for cols in columns(depth):
                b, k, one = buoy[:, whole, cols], stiff[:, whole, cols], s1[:, rows, cols]
                values = []
                for s in range(parts):
                    lap, grad = face_terms(
                        planes_of(low_ref, s, part, cols), planes_of(high_ref, s, part, cols), slab
                    )
                    values.append(b * lap + one * grad)
                source = values[0]
                for s in range(1, parts):
                    source = jnp.where(base == s, values[s], source)
                for s in range(parts):
                    if s == 0:
                        scale = jnp.where(base == 0, 0.0, pert_own[:, whole, cols])
                    else:
                        scale = scales[s - 1][:, rows, cols]
                    value = partial[s, :, mine, cols] + k * values[s] + scale * source
                    if s == 0:
                        own[:, part, cols] = value
                    else:
                        others[s - 1, :, part, cols] = value
            return 0

        lax.fori_loop(0, count // SUB, body, 0, unroll=2)

    pl.when(info[EVEN] == 1)(lambda: loop(True))
    pl.when(info[EVEN] == 0)(lambda: loop(False))


def call(kernel, info, args, outs, scratch=(), flops=0, space=None):
    vmem = pl.BlockSpec(memory_space=pltpu.VMEM)
    source = pl.BlockSpec(memory_space=space or pltpu.VMEM)
    outs = [jax.ShapeDtypeStruct(o, jnp.float32) for o in outs]
    size = flops = 1024 if TINY else sum(4 * a.size for a in args) + sum(4 * o.size for o in outs)
    return pl.pallas_call(
        kernel,
        name=kernel.func.__name__,
        out_shape=outs,
        in_specs=[pl.BlockSpec(memory_space=pltpu.SMEM)] + [source] * len(args),
        out_specs=[vmem] * len(outs),
        scratch_shapes=list(scratch),
        compiler_params=pltpu.CompilerParams(vmem_limit_bytes=12 << 20),
        cost_estimate=pl.CostEstimate(flops=flops, bytes_accessed=size, transcendentals=0),
    )(info, *args)


def lay_kernel(count, rows, *refs):
    pieces, result, sems = refs[:count], refs[-2], refs[-1]
    copies = []
    for number, piece in enumerate(pieces):
        target = result.at[:, pl.ds(pl.multiple_of(rows[number], SUB), piece.shape[1]), :]
        copy = pltpu.make_async_copy(piece, target, sems.at[number])
        copy.start()
        copies.append(copy)
    for copy in copies:
        copy.wait()


def lay(pieces, result, shape):
    rows = jnp.stack([row for row, _ in pieces]).astype(jnp.int32)
    pieces = [piece for _, piece in pieces]
    hbm = pl.BlockSpec(memory_space=pltpu.HBM)
    given = [] if result is None else [result]
    return pl.pallas_call(
        functools.partial(lay_kernel, len(pieces)),
        name="lay_kernel",
        out_shape=jax.ShapeDtypeStruct(shape, jnp.float32),
        in_specs=[pl.BlockSpec(memory_space=pltpu.SMEM)]
        + [pl.BlockSpec(memory_space=pltpu.VMEM)] * len(pieces)
        + [hbm] * len(given),
        out_specs=hbm,
        scratch_shapes=[pltpu.SemaphoreType.DMA((len(pieces),))],
        input_output_aliases={1 + len(pieces): 0} if given else {},
        compiler_params=pltpu.CompilerParams(vmem_limit_bytes=12 << 20),
    )(rows, *pieces, *given)


def after(value, *others):
    return lax.optimization_barrier((value, *others))[0]


def on_device(field_before, field_now, stiffness, buoyancy, perturbation):
    parts, count = lax.axis_size("probe"), lax.axis_size("space")
    part, place = lax.axis_index("probe"), lax.axis_index("space")
    before, now, pert = field_before[0], field_now[0], perturbation[0]
    slab, height, depth = now.shape
    far = parts - 1
    core = height // parts
    rim = 2 * REACH
    width = min(height, core + (2 if parts > 2 else 1) * rim)
    half = SUB * (core // SUB * HALF[0] // HALF[1])
    halves = (half, core - half)
    split = half + width - core
    chunks = (split, width - split)

    def window(p):
        return jnp.clip(core * p - rim, 0, height - width)

    even = place % 2 == 0
    info = jnp.stack(
        [window(part), even, place == 0, place == count - 1, part, core * part - window(part)]
        + [window((part + s) % parts) for s in range(1, parts)]
    ).astype(jnp.int32)

    inner_pairs = [(i, i ^ 1) for i in range(count)]
    outer_pairs = [(i, ((i + 1) ^ 1) - 1) for i in range(1, count - 1)]

    def swap(stack, pairs, from_end):
        if slab > REACH:
            stack = lax.dynamic_slice_in_dim(stack, jnp.where(from_end, slab - REACH, 0), REACH, axis=1)
        return lax.ppermute(stack, "space", pairs)

    def inside(stack):
        return swap(stack, inner_pairs, even)

    def outside(stack):
        return swap(stack, outer_pairs, jnp.logical_not(even))

    def turn(field, s):
        return lax.ppermute(field, "probe", [(i, (i + s) % parts) for i in range(parts)])

    def run_pack(args, copies, outs):
        return call(
            functools.partial(pack_kernel, tuple(copies), len(args)),
            info,
            args,
            outs,
            [pltpu.SemaphoreType.DMA((len(copies),))],
            space=pltpu.HBM,
        )

    spans = ((0, split), (split, width - split))
    copies, outs = [], []
    for span in ((0, width),) + spans:
        for f in range(2):
            copies.append((f, 0, span[0], len(outs), f))
        outs.append((2, slab, span[1], depth))
    for s in range(1, parts):
        for span in spans:
            copies.append((1, s, span[0], len(outs), 0))
            outs.append((1, slab, span[1], depth))
    face, face_a, face_b, *turning = run_pack(
        [pltpu.with_memory_space_constraint(field, pltpu.HBM) for field in (buoyancy, now)], copies, outs
    )

    out_own = [outside(face_a)]
    in_own = inside(face)
    nows = [[turn(turning[2 * (s - 1)], s) for s in range(1, parts)]]
    out_far = [[outside(field) for field in nows[0]]]
    in_far = [[inside(field) for field in nows[0]]]
    nows.append([turn(after(turning[2 * s - 1], *in_far[0]), s) for s in range(1, parts)])
    out_own.append(outside(after(face_b, *nows[0])))

    scr = pltpu.VMEM((slab, depth // LANES, width + 2 * SUB, LANES), jnp.float32)
    wide = (slab, width, depth)
    cells = slab * width * depth
    s1, s2, s3 = call(functools.partial(slope_kernel, width), info, (after(buoyancy, in_own, out_own[0]),), [wide] * 3, [scr], 33 * cells)

    copies, outs = [], []
    for s in range(1, parts):
        for span in spans:
            for f in range(2):
                copies.append((f, s, span[0], len(outs), f))
            outs.append((2, slab, span[1], depth))
    packed = run_pack((after(before, *nows[0]), pert), copies, outs)
    pairs = [[turn(packed[2 * (s - 1)], s) for s in range(1, parts)]]

    image, along = call(
        functools.partial(own_kernel, width), info, (now, buoyancy, s2, s3), [wide] * 2, [scr], 60 * cells
    )
    images, alongs = [image], [along]

    wholes = []
    for s in range(1, parts):
        image, along, whole = call(
            functools.partial(far_kernel, width, split),
            info,
            (nows[0][s - 1], nows[1][s - 1], buoyancy, s2, s3),
            [wide] * 3,
            [scr],
            60 * cells,
        )
        images.append(image)
        alongs.append(along)
        wholes.append(whole)
    sent = [after(field, images[-1]) for field in nows[1]]
    out_far.append([outside(field) for field in sent])
    in_far.append([inside(field) for field in sent])
    pairs.append([turn(after(packed[2 * (s - 1) + 1], images[-1]), s) for s in range(1, parts)])

    carried = ()
    faces = []
    for c in range(2):
        args = (
            [in_own, out_own[c]] + in_far[c] + out_far[c] + [now, before, pert, stiffness, buoyancy, s1]
            + wholes + pairs[c] + images + alongs
        )
        outs = [(parts, slab, width, depth), wide] + [wide] * far
        *carried, face = call(
            functools.partial(finish_kernel, parts, spans[c][0], spans[c][1], c * half, c == 1),
            info,
            (*args, *carried),
            outs + [(parts, slab, halves[c], depth)],
            (),
            45 * parts * spans[c][1] * slab * depth,
        )
        faces.append(face)
    following, slope, *scales = carried

    out_ends = [outside(face) for face in faces]
    in_ends = [inside(face) for face in faces]
    (partial,) = call(
        functools.partial(start_kernel, parts, width, core),
        info,
        (following, now, pert, stiffness, buoyancy, slope, s2, s3, *wholes, *scales),
        [(parts, slab, core, depth)],
        [scr] * parts,
        70 * parts * cells,
    )
    pieces = []
    for c in range(2):
        own, others = call(
            functools.partial(end_kernel, parts, c * half),
            info,
            (in_ends[c], out_ends[c], partial, pert, stiffness, buoyancy, slope, *scales),
            [(slab, halves[c], depth), (far, slab, halves[c], depth)],
            (),
            25 * parts * slab * halves[c] * depth,
        )
        pieces.append((core * part + c * half, own))
        for s in range(1, parts):
            row = core * ((part + s) % parts) + c * half
            pieces.append((row, turn(others[s - 1], parts - s)))
    result = lay(pieces[:-far], None, now.shape)
    result = lay(pieces[-far:], result, now.shape)
    return result[None]


def solution(mesh):
    placed = (
        P("probe", "space", None, None),
        P("probe", "space", None, None),
        P("space", None, None),
        P("space", None, None),
        P("probe", "space", None, None),
    )
    return jax.shard_map(
        on_device,
        mesh=mesh,
        in_specs=placed,
        out_specs=P("probe", "space", None, None),
        check_vma=False,
    )
```

```python
import functools

import jax
import jax.numpy as jnp
from jax import lax
from jax.experimental import pallas as pl
from jax.experimental.pallas import tpu as pltpu
from jax.sharding import PartitionSpec as P

STEPS = 2
REACH = 4
SUB = 8
LANES = 128
HALF = (1, 2)
TINY = True

second_coeffs = (8.0 / 5.0, -1.0 / 5.0, 8.0 / 315.0, -1.0 / 560.0)
first_coeffs = (4.0 / 5.0, -1.0 / 5.0, 4.0 / 105.0, -1.0 / 280.0)
centre_coeff = -205.0 / 72.0


def aligned(row):
    return pl.ds(pl.multiple_of(row, SUB), SUB)


def total_of(terms):
    total = None
    for term in terms:
        total = term if total is None else total + term
    return total


def pad_rows(scr, load, width):
    planes, halves = scr.shape[0], scr.shape[1]
    zero = jnp.zeros((planes, SUB, LANES), jnp.float32)
    for h in range(halves):
        scr[:, h, pl.ds(0, SUB), :] = zero
        scr[:, h, pl.ds(width + SUB, SUB), :] = zero

    def body(i, _):
        value = load(SUB * i)
        for h in range(halves):
            scr[:, h, aligned(SUB * (i + 1)), :] = value[:, :, h * LANES:(h + 1) * LANES]
        return 0

    lax.fori_loop(0, width // SUB, body, 0)


def local_terms(scr, row, h, lane, with_second=True):
    halves = scr.shape[1]
    here = [scr[:, j, aligned(row + SUB), :] for j in range(halves)]
    centre = here[h]
    slab = centre.shape[0]
    grads = ([], [])
    laps = []
    for k in range(1, REACH + 1):
        up = pltpu.roll(centre, LANES - k, 2)
        down = pltpu.roll(centre, k, 2)
        above = pltpu.roll(here[h + 1], LANES - k, 2) if h + 1 < halves else 0.0
        below = pltpu.roll(here[h - 1], k, 2) if h > 0 else 0.0
        up = jnp.where(lane < LANES - k, up, above)
        down = jnp.where(lane >= k, down, below)
        right = scr[:, h, pl.ds(row + SUB + k, SUB), :]
        left = scr[:, h, pl.ds(row + SUB - k, SUB), :]
        grads[0].append(first_coeffs[k - 1] * (right - left))
        grads[1].append(first_coeffs[k - 1] * (up - down))
        if with_second:
            laps.append(second_coeffs[k - 1] * ((right + left) + (up + down)))
    planes = []
    plane_laps = []
    for p in range(slab):
        first, second = [], []
        for k in range(1, REACH + 1):
            high = centre[p + k] if p + k < slab else None
            low = centre[p - k] if p >= k else None
            if high is not None and low is not None:
                first.append(first_coeffs[k - 1] * (high - low))
                second.append(second_coeffs[k - 1] * (high + low))
            elif high is not None:
                first.append(first_coeffs[k - 1] * high)
                second.append(second_coeffs[k - 1] * high)
            elif low is not None:
                first.append(-first_coeffs[k - 1] * low)
                second.append(second_coeffs[k - 1] * low)
        planes.append(total_of(first))
        plane_laps.append(total_of(second))
    along = jnp.stack(planes)
    lap = None
    if with_second:
        lap = total_of(laps + [(3.0 * centre_coeff) * centre, jnp.stack(plane_laps)])
    return centre, lap, along, total_of(grads[0]), total_of(grads[1])


def face_terms(low, high, slab, with_second=True):
    laps, grads = [], []
    for p in range(slab):
        first, second = [], []
        for k in range(1, REACH + 1):
            if p + k >= slab:
                plane = high[p + k - slab]
                first.append(first_coeffs[k - 1] * plane)
                second.append(second_coeffs[k - 1] * plane)
            if p - k < 0:
                plane = low[REACH + p - k]
                first.append(-first_coeffs[k - 1] * plane)
                second.append(second_coeffs[k - 1] * plane)
        zero = jnp.zeros_like(low[0])
        grads.append(total_of(first) if first else zero)
        laps.append(total_of(second) if second else zero)
    return (jnp.stack(laps) if with_second else None), jnp.stack(grads)


def lane_index(slab):
    return lax.broadcasted_iota(jnp.int32, (slab, SUB, LANES), 2)


def columns(depth):
    return [slice(h * LANES, (h + 1) * LANES) for h in range(depth // LANES)]


START, EVEN, FIRST, LAST, PART, OFFSET, OTHERS = range(7)


def pack_kernel(copies, count, info, *refs):
    sources, outs, sems = refs[:count], refs[count:-1], refs[-1]
    started = []
    for number, (source, who, row, out, at) in enumerate(copies):
        begin = info[START] if who == 0 else info[OTHERS + who - 1]
        target = outs[out].at[at]
        rows = pl.ds(pl.multiple_of(begin + row, SUB), target.shape[1])
        copy = pltpu.make_async_copy(sources[source].at[:, rows, :], target, sems.at[number])
        copy.start()
        started.append(copy)
    for copy in started:
        copy.wait()


def slope_kernel(width, info, buoy, s1, s2, s3, scr):
    slab = scr.shape[0]
    pad_rows(scr, lambda row: buoy[:, aligned(info[START] + row), :] - 1.0, width)
    lane = lane_index(slab)

    def body(i, _):
        for h, cols in enumerate(columns(buoy.shape[2])):
            _, _, one, two, three = local_terms(scr, SUB * i, h, lane, False)
            s1[:, aligned(SUB * i), cols] = one
            s2[:, aligned(SUB * i), cols] = two
            s3[:, aligned(SUB * i), cols] = three
        return 0

    lax.fori_loop(0, width // SUB, body, 0, unroll=1 if width % (2 * SUB) else 2)


def local_loop(width, start, depth, buoy, s2, s3, image, along, scr):
    lane = lane_index(scr.shape[0])

    def body(i, _):
        rows = aligned(SUB * i)
        for h, cols in enumerate(columns(depth)):
            _, lap, one, two, three = local_terms(scr, SUB * i, h, lane)
            b = buoy[:, aligned(start + SUB * i), cols]
            image[:, rows, cols] = b * lap + s2[:, rows, cols] * two + s3[:, rows, cols] * three
            along[:, rows, cols] = one
        return 0

    lax.fori_loop(0, width // SUB, body, 0, unroll=1 if width % (2 * SUB) else 2)


def own_kernel(width, info, now, buoy, s2, s3, image, along, scr):
    pad_rows(scr, lambda row: now[:, aligned(info[START] + row), :], width)
    local_loop(width, info[START], now.shape[2], buoy, s2, s3, image, along, scr)


def far_kernel(width, split, info, now_a, now_b, buoy, s2, s3, image, along, whole, scr):
    halves = scr.shape[1]
    zero = jnp.zeros((scr.shape[0], SUB, LANES), jnp.float32)
    for h in range(halves):
        scr[:, h, pl.ds(0, SUB), :] = zero
        scr[:, h, pl.ds(width + SUB, SUB), :] = zero
    for ref, first in ((now_a, 0), (now_b, split)):

        def body(i, _):
            value = ref[0, :, aligned(SUB * i), :]
            whole[:, aligned(first + SUB * i), :] = value
            for h in range(halves):
                scr[:, h, aligned(first + SUB * (i + 1)), :] = value[:, :, h * LANES:(h + 1) * LANES]
            return 0

        lax.fori_loop(0, ref.shape[2] // SUB, body, 0)
    local_loop(width, info[START], buoy.shape[2], buoy, s2, s3, image, along, scr)


def planes_of(ref, index, rows, cols):
    return [ref[index, q, rows, cols] for q in range(REACH)]


def finish_kernel(parts, first_row, count, face_row, again, info, *refs):
    refs = list(refs)

    def take(n):
        got = refs[:n]
        del refs[:n]
        return got

    far = parts - 1
    in_own, out_own = take(2)
    ins, outs = take(far), take(far)
    now_own, before_own, pert_own, stiff, buoy, s1 = take(6)
    nows, pairs = take(far), take(far)
    images, alongs = take(parts), take(parts)
    earlier = take(2 + far) if again else ()
    following, slope, *scales, faces = refs
    start, base, offset = info[START], info[PART], info[OFFSET]
    first, last = info[FIRST] == 1, info[LAST] == 1
    slab, depth = s1.shape[0], s1.shape[2]

    def loop(even):
        def sides(index, inner, inner_rows, outer, outer_rows, cols):
            inside = planes_of(inner, index, inner_rows, cols)
            outside = planes_of(outer, index, outer_rows, cols)
            return (outside, inside) if even else (inside, outside)

        def body(i, _):
            part = aligned(SUB * i)
            rows = aligned(first_row + SUB * i)
            whole = aligned(start + first_row + SUB * i)
            for cols in columns(depth):
                low, high = sides(0, in_own, rows, out_own, part, cols)
                low = [jnp.where(first, 0.0, plane - 1.0) for plane in low]
                high = [jnp.where(last, 0.0, plane - 1.0) for plane in high]
                one = s1[:, rows, cols] + face_terms(low, high, slab, False)[1]
                slope[:, rows, cols] = one
                b, k = buoy[:, whole, cols], stiff[:, whole, cols]
                values = []
                for s in range(parts):
                    if s == 0:
                        low, high = sides(1, in_own, rows, out_own, part, cols)
                    else:
                        low, high = sides(0, ins[s - 1], part, outs[s - 1], part, cols)
                    lap, grad = face_terms(low, high, slab)
                    values.append(images[s][:, rows, cols] + b * lap + one * (alongs[s][:, rows, cols] + grad))
                source = values[0]
                for s in range(1, parts):
                    source = jnp.where(base == s, values[s], source)
                for s in range(parts):
                    if s == 0:
                        now, before = now_own[:, whole, cols], before_own[:, whole, cols]
                        scale = jnp.where(base == 0, 0.0, pert_own[:, whole, cols])
                    else:
                        now, before = nows[s - 1][:, rows, cols], pairs[s - 1][0, :, part, cols]
                        scale = jnp.where(base == s, 0.0, pairs[s - 1][1, :, part, cols])
                        scales[s - 1][:, rows, cols] = scale
                    following[s, :, rows, cols] = 2.0 * now - before + k * values[s] + scale * source
            return 0

        lax.fori_loop(0, count // SUB, body, 0, unroll=2)

    pl.when(info[EVEN] == 1)(lambda: loop(True))
    pl.when(info[EVEN] == 0)(lambda: loop(False))

    def keep(i, _):
        for source, target in zip(earlier, (following, slope, *scales)):
            rows = aligned(SUB * i)
            if len(source.shape) == 4:
                target[:, :, rows, :] = source[:, :, rows, :]
            else:
                target[:, rows, :] = source[:, rows, :]
        return 0

    if again:
        lax.fori_loop(0, first_row // SUB, keep, 0, unroll=3)

    def send(i, _):
        faces[:, :, aligned(SUB * i), :] = following[:, :, aligned(offset + face_row + SUB * i), :]
        return 0

    lax.fori_loop(0, faces.shape[2] // SUB, send, 0, unroll=2)


def start_kernel(parts, width, core, info, *refs):
    field, now_own, pert_own, stiff, buoy, s1, s2, s3 = refs[:8]
    nows, scales = refs[8:8 + parts - 1], refs[8 + parts - 1:8 + 2 * (parts - 1)]
    partial, scrs = refs[8 + 2 * (parts - 1)], refs[9 + 2 * (parts - 1):]
    start, base, offset = info[START], info[PART], info[OFFSET]
    for s in range(parts):
        pad_rows(scrs[s], lambda row, s=s: field[s, :, aligned(row), :], width)
    lane = lane_index(s1.shape[0])

    def body(i, _):
        out = aligned(SUB * i)
        rows = aligned(offset + SUB * i)
        whole = aligned(start + offset + SUB * i)
        for h, cols in enumerate(columns(s1.shape[2])):
            slopes = [ref[:, rows, cols] for ref in (s1, s2, s3)]
            b, k = buoy[:, whole, cols], stiff[:, whole, cols]
            centres, values = [], []
            for s in range(parts):
                centre, lap, one, two, three = local_terms(scrs[s], offset + SUB * i, h, lane)
                centres.append(centre)
                values.append(b * lap + slopes[0] * one + slopes[1] * two + slopes[2] * three)
            source = values[0]
            for s in range(1, parts):
                source = jnp.where(base == s, values[s], source)
            for s in range(parts):
                if s == 0:
                    now = now_own[:, whole, cols]
                    scale = jnp.where(base == 0, 0.0, pert_own[:, whole, cols])
                else:
                    now, scale = nows[s - 1][:, rows, cols], scales[s - 1][:, rows, cols]
                partial[s, :, out, cols] = 2.0 * centres[s] - now + k * values[s] + scale * source
        return 0

    lax.fori_loop(0, core // SUB, body, 0)


def end_kernel(parts, first_row, info, *refs):
    inner, outer, partial, pert_own, stiff, buoy, s1 = refs[:7]
    scales = refs[7:7 + parts - 1]
    own, others = refs[-2:]
    start, base, offset = info[START], info[PART], info[OFFSET]
    slab, depth, count = s1.shape[0], s1.shape[2], inner.shape[2]

    def loop(even):
        low_ref, high_ref = (outer, inner) if even else (inner, outer)

        def body(i, _):
            part = aligned(SUB * i)
            mine = aligned(first_row + SUB * i)
            rows = aligned(offset + first_row + SUB * i)
            whole = aligned(start + offset + first_row + SUB * i)
            for cols in columns(depth):
                b, k, one = buoy[:, whole, cols], stiff[:, whole, cols], s1[:, rows, cols]
                values = []
                for s in range(parts):
                    lap, grad = face_terms(
                        planes_of(low_ref, s, part, cols), planes_of(high_ref, s, part, cols), slab
                    )
                    values.append(b * lap + one * grad)
                source = values[0]
                for s in range(1, parts):
                    source = jnp.where(base == s, values[s], source)
                for s in range(parts):
                    if s == 0:
                        scale = jnp.where(base == 0, 0.0, pert_own[:, whole, cols])
                    else:
                        scale = scales[s - 1][:, rows, cols]
                    value = partial[s, :, mine, cols] + k * values[s] + scale * source
                    if s == 0:
                        own[:, part, cols] = value
                    else:
                        others[s - 1, :, part, cols] = value
            return 0

        lax.fori_loop(0, count // SUB, body, 0, unroll=2)

    pl.when(info[EVEN] == 1)(lambda: loop(True))
    pl.when(info[EVEN] == 0)(lambda: loop(False))


def call(kernel, info, args, outs, scratch=(), flops=0, space=None):
    vmem = pl.BlockSpec(memory_space=pltpu.VMEM)
    source = pl.BlockSpec(memory_space=space or pltpu.VMEM)
    outs = [jax.ShapeDtypeStruct(o, jnp.float32) for o in outs]
    size = flops = 1024 if TINY else sum(4 * a.size for a in args) + sum(4 * o.size for o in outs)
    return pl.pallas_call(
        kernel,
        name=kernel.func.__name__,
        out_shape=outs,
        in_specs=[pl.BlockSpec(memory_space=pltpu.SMEM)] + [source] * len(args),
        out_specs=[vmem] * len(outs),
        scratch_shapes=list(scratch),
        compiler_params=pltpu.CompilerParams(vmem_limit_bytes=12 << 20),
        cost_estimate=pl.CostEstimate(flops=flops, bytes_accessed=size, transcendentals=0),
    )(info, *args)


def lay_kernel(count, rows, *refs):
    pieces, result, sems = refs[:count], refs[-2], refs[-1]
    copies = []
    for number, piece in enumerate(pieces):
        target = result.at[:, pl.ds(pl.multiple_of(rows[number], SUB), piece.shape[1]), :]
        copy = pltpu.make_async_copy(piece, target, sems.at[number])
        copy.start()
        copies.append(copy)
    for copy in copies:
        copy.wait()


def lay(pieces, result, shape):
    rows = jnp.stack([row for row, _ in pieces]).astype(jnp.int32)
    pieces = [piece for _, piece in pieces]
    hbm = pl.BlockSpec(memory_space=pltpu.HBM)
    given = [] if result is None else [result]
    return pl.pallas_call(
        functools.partial(lay_kernel, len(pieces)),
        name="lay_kernel",
        out_shape=jax.ShapeDtypeStruct(shape, jnp.float32),
        in_specs=[pl.BlockSpec(memory_space=pltpu.SMEM)]
        + [pl.BlockSpec(memory_space=pltpu.VMEM)] * len(pieces)
        + [hbm] * len(given),
        out_specs=hbm,
        scratch_shapes=[pltpu.SemaphoreType.DMA((len(pieces),))],
        input_output_aliases={1 + len(pieces): 0} if given else {},
        compiler_params=pltpu.CompilerParams(vmem_limit_bytes=12 << 20),
    )(rows, *pieces, *given)


def after(value, *others):
    return lax.optimization_barrier((value, *others))[0]


def on_device(field_before, field_now, stiffness, buoyancy, perturbation):
    parts, count = lax.axis_size("probe"), lax.axis_size("space")
    part, place = lax.axis_index("probe"), lax.axis_index("space")
    before, now, pert = field_before[0], field_now[0], perturbation[0]
    slab, height, depth = now.shape
    far = parts - 1
    core = height // parts
    rim = 2 * REACH
    width = min(height, core + (2 if parts > 2 else 1) * rim)
    half = SUB * (core // SUB * HALF[0] // HALF[1])
    halves = (half, core - half)
    split = half + width - core
    chunks = (split, width - split)

    def window(p):
        return jnp.clip(core * p - rim, 0, height - width)

    even = place % 2 == 0
    info = jnp.stack(
        [window(part), even, place == 0, place == count - 1, part, core * part - window(part)]
        + [window((part + s) % parts) for s in range(1, parts)]
    ).astype(jnp.int32)

    inner_pairs = [(i, i ^ 1) for i in range(count)]
    outer_pairs = [(i, ((i + 1) ^ 1) - 1) for i in range(1, count - 1)]

    def swap(stack, pairs, from_end):
        if slab > REACH:
            stack = lax.dynamic_slice_in_dim(stack, jnp.where(from_end, slab - REACH, 0), REACH, axis=1)
        return lax.ppermute(stack, "space", pairs)

    def inside(stack):
        return swap(stack, inner_pairs, even)

    def outside(stack):
        return swap(stack, outer_pairs, jnp.logical_not(even))

    def turn(field, s):
        return lax.ppermute(field, "probe", [(i, (i + s) % parts) for i in range(parts)])

    def run_pack(args, copies, outs):
        return call(
            functools.partial(pack_kernel, tuple(copies), len(args)),
            info,
            args,
            outs,
            [pltpu.SemaphoreType.DMA((len(copies),))],
            space=pltpu.HBM,
        )

    spans = ((0, split), (split, width - split))
    copies, outs = [], []
    for span in ((0, width),) + spans:
        for f in range(2):
            copies.append((f, 0, span[0], len(outs), f))
        outs.append((2, slab, span[1], depth))
    for s in range(1, parts):
        for span in spans:
            copies.append((1, s, span[0], len(outs), 0))
            outs.append((1, slab, span[1], depth))
    face, face_a, face_b, *turning = run_pack(
        [pltpu.with_memory_space_constraint(field, pltpu.HBM) for field in (buoyancy, now)], copies, outs
    )

    out_own = [outside(face_a)]
    in_own = inside(face)
    nows = [[turn(turning[2 * (s - 1)], s) for s in range(1, parts)]]
    out_far = [[outside(field) for field in nows[0]]]
    in_far = [[inside(field) for field in nows[0]]]
    nows.append([turn(after(turning[2 * s - 1], *in_far[0]), s) for s in range(1, parts)])
    out_own.append(outside(after(face_b, *nows[0])))

    scr = pltpu.VMEM((slab, depth // LANES, width + 2 * SUB, LANES), jnp.float32)
    wide = (slab, width, depth)
    cells = slab * width * depth
    s1, s2, s3 = call(functools.partial(slope_kernel, width), info, (after(buoyancy, in_own, out_own[0]),), [wide] * 3, [scr], 33 * cells)

    copies, outs = [], []
    for s in range(1, parts):
        for span in spans:
            for f in range(2):
                copies.append((f, s, span[0], len(outs), f))
            outs.append((2, slab, span[1], depth))
    packed = run_pack((after(before, *nows[0]), pert), copies, outs)
    pairs = [[turn(packed[2 * (s - 1)], s) for s in range(1, parts)]]

    image, along = call(
        functools.partial(own_kernel, width), info, (now, buoyancy, s2, s3), [wide] * 2, [scr], 60 * cells
    )
    images, alongs = [image], [along]

    wholes = []
    for s in range(1, parts):
        image, along, whole = call(
            functools.partial(far_kernel, width, split),
            info,
            (nows[0][s - 1], nows[1][s - 1], buoyancy, s2, s3),
            [wide] * 3,
            [scr],
            60 * cells,
        )
        images.append(image)
        alongs.append(along)
        wholes.append(whole)
    sent = [after(field, images[-1]) for field in nows[1]]
    out_far.append([outside(field) for field in sent])
    in_far.append([inside(field) for field in sent])
    pairs.append([turn(after(packed[2 * (s - 1) + 1], images[-1]), s) for s in range(1, parts)])

    carried = ()
    faces = []
    for c in range(2):
        args = (
            [in_own, out_own[c]] + in_far[c] + out_far[c] + [now, before, pert, stiffness, buoyancy, s1]
            + wholes + pairs[c] + images + alongs
        )
        outs = [(parts, slab, width, depth), wide] + [wide] * far
        *carried, face = call(
            functools.partial(finish_kernel, parts, spans[c][0], spans[c][1], c * half, c == 1),
            info,
            (*args, *carried),
            outs + [(parts, slab, halves[c], depth)],
            (),
            45 * parts * spans[c][1] * slab * depth,
        )
        faces.append(face)
    following, slope, *scales = carried

    out_ends = [outside(face) for face in faces]
    in_ends = [inside(face) for face in faces]
    (partial,) = call(
        functools.partial(start_kernel, parts, width, core),
        info,
        (following, now, pert, stiffness, buoyancy, slope, s2, s3, *wholes, *scales),
        [(parts, slab, core, depth)],
        [scr] * parts,
        70 * parts * cells,
    )
    pieces = []
    for c in range(2):
        own, others = call(
            functools.partial(end_kernel, parts, c * half),
            info,
            (in_ends[c], out_ends[c], partial, pert, stiffness, buoyancy, slope, *scales),
            [(slab, halves[c], depth), (far, slab, halves[c], depth)],
            (),
            25 * parts * slab * halves[c] * depth,
        )
        pieces.append((core * part + c * half, own))
        for s in range(1, parts):
            row = core * ((part + s) % parts) + c * half
            pieces.append((row, turn(others[s - 1], parts - s)))
    result = lay(pieces[:-far], None, now.shape)
    result = lay(pieces[-far:], result, now.shape)
    return result[None]


def solution(mesh):
    placed = (
        P("probe", "space", None, None),
        P("probe", "space", None, None),
        P("space", None, None),
        P("space", None, None),
        P("probe", "space", None, None),
    )
    return jax.shard_map(
        on_device,
        mesh=mesh,
        in_specs=placed,
        out_specs=P("probe", "space", None, None),
        check_vma=False,
    )
```
